256 devices in a mesh: tiles: 128 (over z, y_hi, x, core), cls: 2 (over y_lo).
Axes of the slice: x: 4, y: 4 (y_hi: 2, y_lo: 2; y = y_hi * 2 + y_lo), z: 8, core: 2. Of those that a mesh axis runs over, the one named last changes fastest.
Arguments:
- scaling: float32 [4, 2048, 8192], P('cls', 'tiles'), may hold values from 0.5 to 2
- source: float32 [4, 2048, 8192], P('cls', 'tiles'), may hold values from 0.3 to 4.5
- speed: float32 [4, 2048, 8192], P('cls', 'tiles'), may hold values from 0.3 to 1.5
- tile_mask: int32 [8, 32], replicated, may hold values from 0 to 1, as said below
- target: float32 [4], P('cls'), may hold values from 0.5 to 2
Outputs:
- heat_field: float32 [4, 2048, 8192], P('cls', 'tiles')
- flow_scaling: float32 [4, 2048, 8192], P('cls', 'tiles')
The draws below stay inside these ranges and needn't reach their ends.
Inputs may be any that keep to these rules, and one draw needn't show every extreme that they name: `tile_mask`: 1 marks a land tile, 0 a sea tile; every row of tiles holds at least one land tile.
All inputs are finite; a program needn't handle non-finite values.
Results may differ from the reference program's by a relative error of at most 0.0001.
Values sent between devices are 32-bit elements; how exact they have to be, the bound alone decides.
A program may use at most 128 MiB of HBM per device.

```python
import math
import jax
import jax.numpy as jnp
from jax import lax

TS = 256
GC = 32
CLS = 4
VCYC = 1
NU = 2
J1 = 8
RASTER_ROWS = 2048
TILE_ROWS = 8
RASTER_COLS = 8192


def draw_source(key, part):
    row_index = jnp.arange(RASTER_ROWS, dtype=jnp.float32)[None, :, None]
    ramp = 1.0 + 2.0 * row_index / max(RASTER_ROWS - 1, 1)
    base = jnp.exp(jax.random.uniform(key, (CLS, RASTER_ROWS, RASTER_COLS), jnp.float32, math.log(0.3), math.log(1.5)))
    return base * ramp


def draw_tile_mask(key, part):
    bits_key = jax.random.fold_in(key, 11)
    column_key = jax.random.fold_in(key, 23)
    drawn = jax.random.randint(bits_key, (TILE_ROWS, GC), 0, 10)
    random_land = (drawn < 7).astype(jnp.int32)
    forced_column = jax.random.randint(column_key, (TILE_ROWS, 1), 0, GC)
    forced_land = (jnp.arange(GC, dtype=jnp.int32)[None, :] == forced_column).astype(jnp.int32)
    return jnp.maximum(random_land, forced_land)


def steps_of(own_key, dims, cuts, smallest, top_value):
    gain = 1.0
    for position, blocks in cuts:
        draws = jax.random.uniform(jax.random.fold_in(jax.random.fold_in(own_key, 6), position), (blocks,), jnp.float32, smallest / len(cuts), top_value / len(cuts))
        gain = gain * jnp.repeat(jnp.exp(draws), dims[position] // blocks).reshape((-1,) + (1,) * (len(dims) - 1 - position))
    return gain


def setup_inputs(seed: int = 0) -> dict:
    keys = jax.random.split(jax.random.key(seed), 6)
    scaling = jnp.clip(jnp.exp(math.log(2.0) - 1.3862944 * jax.random.uniform(keys[0], (CLS, RASTER_ROWS, RASTER_COLS), jnp.float32) ** steps_of(keys[0], (CLS, RASTER_ROWS, RASTER_COLS), ((0, 2), (1, 128)), -0.2, 0.2)), 0.5, 2.0)
    source = draw_source(jax.random.fold_in(keys[5], 71), 0)
    speed = jnp.clip(jnp.exp(math.log(1.5) - 1.60943787 * jax.random.uniform(keys[2], (CLS, RASTER_ROWS, RASTER_COLS), jnp.float32) ** steps_of(keys[2], (CLS, RASTER_ROWS, RASTER_COLS), ((0, 2), (1, 128)), -0.2, 0.2)), 0.3, 1.5)
    tile_mask = draw_tile_mask(jax.random.fold_in(keys[5], 71), 0)
    target = jnp.clip(jnp.exp(math.log(2.0) - 1.3862944 * jax.random.uniform(keys[4], (CLS,), jnp.float32) ** steps_of(keys[4], (CLS,), ((0, 2),), -0.2, 0.2)), 0.5, 2.0)
    return dict(scaling=scaling, source=source, speed=speed, tile_mask=tile_mask, target=target)


OMEGA_DAMP = 0.8
FINE_STRENGTH = 8.0
COARSE_SCALE = 16.0
COARSE_STRENGTH = 32.0
FLOOR_LEVEL = 0.25
directions = ((-1, 0, 1.0), (1, 0, 1.0), (0, -1, 1.0), (0, 1, 1.0), (-1, -1, 0.5), (-1, 1, 0.5), (1, -1, 0.5), (1, 1, 0.5))


def coefficients(speed_wide, diag_scale, strength):
    row_count = speed_wide.shape[1] - 2
    col_count = speed_wide.shape[2]
    speed_pad = jnp.pad(speed_wide, ((0, 0), (0, 0), (1, 1)))
    near_speed = jnp.zeros((speed_wide.shape[0], row_count, col_count), jnp.float32)
    for row_step, col_step, weight in directions:
        near_speed = near_speed + weight * speed_pad[:, 1 + row_step:1 + row_step + row_count, 1 + col_step:1 + col_step + col_count]
    coupling = strength * speed_wide[:, 1:row_count + 1, :]
    diagonal = diag_scale + coupling * near_speed
    return speed_pad, coupling, diagonal


def operate(field_wide, coeffs):
    speed_pad, coupling, diagonal = coeffs
    row_count = field_wide.shape[1] - 2
    col_count = field_wide.shape[2]
    padded = jnp.pad(field_wide, ((0, 0), (0, 0), (1, 1)))
    near_field = jnp.zeros_like(diagonal)
    for row_step, col_step, weight in directions:
        other_speed = speed_pad[:, 1 + row_step:1 + row_step + row_count, 1 + col_step:1 + col_step + col_count]
        other_field = padded[:, 1 + row_step:1 + row_step + row_count, 1 + col_step:1 + col_step + col_count]
        near_field = near_field + weight * other_speed * other_field
    center = field_wide[:, 1:row_count + 1, :]
    return diagonal * center - coupling * near_field, center


def jacobi(field_wide, right_side, land_cells, coeffs):
    applied, center = operate(field_wide, coeffs)
    return land_cells * (center + OMEGA_DAMP * (right_side - applied) / coeffs[2])


def pad_rows(field, width):
    return jnp.pad(field, ((0, 0), (width, width), (0, 0)))


def block_mean(field):
    shaped = field.reshape(field.shape[0], field.shape[1] // 4, 4, field.shape[2] // 4, 4)
    return jnp.mean(shaped, axis=(2, 4))


def block_sum(field):
    shaped = field.reshape(field.shape[0], field.shape[1] // 4, 4, field.shape[2] // 4, 4)
    return jnp.sum(shaped, axis=(2, 4))


def upsample(field):
    return jnp.repeat(jnp.repeat(field, 4, axis=1), 4, axis=2)


def reference(scaling, source, speed, tile_mask, target):
    mask_float = tile_mask.astype(jnp.float32)
    land_cells = jnp.repeat(jnp.repeat(mask_float, TS, 0), TS, 1)[None]
    quarter = TS // 4
    coarse_land = jnp.repeat(jnp.repeat(mask_float, quarter, 0), quarter, 1)[None]

    def solve_class(inputs):
        scaling_one = inputs[0][None]
        speed_one = inputs[1][None]
        fine_coeffs = coefficients(pad_rows(speed_one, 1), 1.0, FINE_STRENGTH)
        coarse_coeffs = coefficients(pad_rows(block_mean(speed_one), 1), COARSE_SCALE, COARSE_STRENGTH)
        field = jnp.zeros_like(scaling_one)
        for cycle_index in range(VCYC):
            for sweep_index in range(NU):
                field = jacobi(pad_rows(field, 1), scaling_one, land_cells, fine_coeffs)
            applied, center = operate(pad_rows(field, 1), fine_coeffs)
            residual = land_cells * (scaling_one - applied)
            coarse_right = block_sum(residual)
            correction = jnp.zeros_like(coarse_right)
            for sweep_index in range(J1):
                correction = jacobi(pad_rows(correction, 1), coarse_right, coarse_land, coarse_coeffs)
            field = field + land_cells * upsample(correction)
            for sweep_index in range(NU):
                field = jacobi(pad_rows(field, 1), scaling_one, land_cells, fine_coeffs)
        return field[0]

    heat_field = lax.map(solve_class, (scaling, speed))
    global_mass = jnp.sum(source)
    cell_total = float(source.size)
    mass_ratio = target * cell_total / global_mass
    flow_scaling = land_cells * source * mass_ratio[:, None, None] / jnp.maximum(heat_field, FLOOR_LEVEL)
    return heat_field, flow_scaling
```

```python
import jax
import jax.numpy as jnp
from jax import lax
from jax.experimental import pallas as pl
from jax.experimental.pallas import tpu as pltpu
from jax.sharding import PartitionSpec as P

MESH = pl.DeviceIdType.MESH
F32 = jnp.float32
BF16 = jnp.bfloat16
FLOOR_LEVEL = 0.25
TS = 256


def kernel(
    ntiles, ncls,
    mask_ref, target_ref, b_in, src_in, k_in,
    heat_out, flow_out,
    KN, BN, SN, KHN, BHN, KL, CL, WL, DG, FL, GL, KH, CH, WH, FH, GH, RS, CK, GQ, ICK, PC, QC, UC, UP, OH, OF, MS, MR,
    sem_in, sem_out, k_send, k_recv, b_send, b_recv, q_send, q_recv, p_send, p_recv, m_send, m_recv,
):
    me = lax.axis_index("tiles")
    cl = lax.axis_index("cls")
    has_prev, has_next = me > 0, me < ntiles - 1
    has_prev2, has_next2 = me > 1, me < ntiles - 2

    sub = lax.broadcasted_iota(jnp.int32, (8, 128), 0)
    lane = lax.broadcasted_iota(jnp.int32, (8, 128), 1)
    s4 = sub & 3
    m0, m3 = s4 == 0, s4 == 3
    half0 = s4 < 2
    side0 = (sub & 1) == 0
    lane0, lane127 = lane == 0, lane == 127
    zero = jnp.zeros((8, 128), F32)

    def rs(x, n):
        return pltpu.roll(x, n % 8, 0)

    def rl(x, n):
        return pltpu.roll(x, n % 128, 1)

    def load_copies(hbm, vmem, base, s):
        return [
            pltpu.make_async_copy(
                hbm.at[c, rt], vmem.at[pl.ds(base, 64), pl.ds(16 * c + 8 * rt, 8), :], sem_in.at[s * 4 + 2 * c + rt]
            )
            for c in range(2)
            for rt in range(2)
        ]

    k_loads = load_copies(k_in, KN, 1, 0)
    b_loads = load_copies(b_in, BN, 0, 1)
    s_loads = load_copies(src_in, SN, 0, 2)
    for copy in k_loads + s_loads + b_loads:
        copy.start()

    low = me % 8
    mid = me // 8 % 2
    high = me // 16
    place = 2 * mid + cl

    def mass_peer(stage, r):
        if stage == 0:
            return {"tiles": me - low + (low + r) % 8, "cls": cl}
        if stage == 1:
            other = (place + r) % 4
            return {"tiles": me + 8 * (other // 2 - mid), "cls": other % 2}
        return {"tiles": me + 16 * ((high + r) % 8 - high), "cls": cl}

    sizes = (8, 4, 8)
    starts = (0, 8, 12)

    barrier = pltpu.get_barrier_semaphore()

    def greet(there):
        pl.semaphore_signal(barrier, inc=1, device_id=there, device_id_type=MESH)

    for step, there in ((-1, has_prev), (1, has_next), (-2, has_prev2), (2, has_next2)):
        @pl.when(there)
        def _():
            greet({"tiles": me + step})
    for stage in range(3):
        for r in range(1, sizes[stage]):
            greet(mass_peer(stage, r))
    one = jnp.int32(1)
    nil = jnp.int32(0)
    greeted = 17
    for there in (has_prev, has_next, has_prev2, has_next2):
        greeted = greeted + jnp.where(there, one, nil)
    pl.semaphore_wait(barrier, greeted)

    def halo_copies(hbm, vmem, base, send, recv):
        to_next, to_prev = [], []
        for c in range(2):
            for half in range(2):
                n = 2 * c + half
                to_next.append(pltpu.make_async_remote_copy(
                    src_ref=hbm.at[c, 1, pl.ds(32 * half, 32), pl.ds(4, 4), :],
                    dst_ref=vmem.at[pl.ds(base, 32), pl.ds(16 * c + 8 * half, 4), :],
                    send_sem=send.at[n], recv_sem=recv.at[n],
                    device_id={"tiles": me + 1}, device_id_type=MESH))
                to_prev.append(pltpu.make_async_remote_copy(
                    src_ref=hbm.at[c, 0, pl.ds(32 * half, 32), pl.ds(0, 4), :],
                    dst_ref=vmem.at[pl.ds(base, 32), pl.ds(16 * c + 8 * half + 4, 4), :],
                    send_sem=send.at[4 + n], recv_sem=recv.at[4 + n],
                    device_id={"tiles": me - 1}, device_id_type=MESH))
        return to_next, to_prev

    k_next, k_prev = halo_copies(k_in, KHN, 1, k_send, k_recv)
    b_next, b_prev = halo_copies(b_in, BHN, 0, b_send, b_recv)

    def start_all(copies, there):
        @pl.when(there)
        def _():
            for copy in copies:
                copy.start()

    def recv_all(copies, there):
        @pl.when(there)
        def _():
            for copy in copies:
                copy.wait_recv()

    def sent_all(copies, there):
        @pl.when(there)
        def _():
            for copy in copies:
                copy.wait_send()

    start_all(k_next, has_next)
    start_all(k_prev, has_prev)
    start_all(b_next, has_next)
    start_all(b_prev, has_prev)

    for n in (0, 65):
        KN[n] = jnp.zeros((32, 128), F32)
        for t in range(4):
            KL[n, t] = zero
            CL[n, t] = zero
            FL[n, t] = zero
            GL[n, t] = zero

    def outside(first, there):
        @pl.when(jnp.logical_not(there))
        def _():
            for c in range(2):
                for half in range(2):
                    row = 16 * c + 8 * half + first
                    KHN[pl.ds(1, 32), pl.ds(row, 4), :] = jnp.zeros((32, 4, 128), F32)
                    BHN[pl.ds(0, 32), pl.ds(row, 4), :] = jnp.zeros((32, 4, 128), F32)

    outside(0, has_prev)
    outside(4, has_next)

    def clear(slot, there):
        @pl.when(jnp.logical_not(there))
        def _():
            PC[slot] = jnp.zeros((16, 8, 128), F32)
            QC[slot] = jnp.zeros((16, 8, 128), F32)

    clear(0, has_prev2)
    clear(1, has_prev)
    clear(3, has_next)
    clear(4, has_next2)
    for q in (0, 17):
        for slot in range(5):
            UC[q, slot] = zero
            UP[q, slot] = zero
        CK[q] = zero

    def mass_copy(stage, r):
        return pltpu.make_async_remote_copy(
            src_ref=MS.at[stage], dst_ref=MR.at[starts[stage] + r],
            send_sem=m_send.at[starts[stage] + r], recv_sem=m_recv.at[starts[stage] + r],
            device_id=mass_peer(stage, r), device_id_type=MESH)

    def mass_start(stage):
        for r in range(1, sizes[stage]):
            mass_copy(stage, r).start()

    def mass_total(stage):
        total = MS[stage]
        for r in range(1, sizes[stage]):
            mass_copy(stage, r).wait_recv()
        for r in range(1, sizes[stage]):
            total = total + MR[starts[stage] + r]
        return total

    for copy in s_loads:
        copy.wait()

    def add_source(n, sums):
        return tuple(
            sums[i] + SN[n * 2 + i // 4, pl.ds(8 * (i % 4), 8), :] for i in range(8)
        )

    sums = lax.fori_loop(0, 32, add_source, (zero,) * 8)
    total = sums[0]
    for part in sums[1:]:
        total = total + part
    MS[0] = total
    mass_start(0)

    row_tile = me * 16 // TS
    prev_tile = jnp.maximum(me * 16 - 1, 0) // TS
    next_tile = jnp.minimum(me * 16 + 16, ntiles * 16 - 1) // TS

    def land(row, block):
        return mask_ref[row, block // 2].astype(F32)

    def along(first, count, sa, finalize, carry, unroll):
        def body(n, carry):
            for i in range(unroll):
                j = first + n * unroll + i
                before, s, right, left = carry
                s_next, a_next = sa(j + 1)
                right_next = [rl(x, 1) for x in a_next]
                left_next = [rl(x, -1) for x in a_next]
                near = [
                    s[t] + jnp.where(lane0, before[t], right[t]) + jnp.where(lane127, left_next[t], left[t])
                    for t in range(len(s))
                ]
                finalize(j, i, near)
                carry = (right, s_next, right_next, left_next)
            return carry

        return lax.fori_loop(0, count // unroll, body, carry)

    def begin(sa, first):
        _, a_before = sa(first - 1)
        s, a = sa(first)
        return ([rl(x, 1) for x in a_before], s, [rl(x, 1) for x in a], [rl(x, -1) for x in a])

    def sums_of(u, up0, down3):
        s = [up0 + u[1], u[0] + u[2], u[1] + u[3], u[2] + down3]
        return s, [u[t] + 0.5 * s[t] for t in range(4)]

    def local_stage(u_at, edge_at, finalize, unroll=4):
        def sa_of(half):
            def sa(j):
                u = u_at(j + 1)
                h = j - 32 * half + 1
                above, below = edge_at(h, 3), edge_at(h, 0)
                if half == 0:
                    below = rs(below, 2)
                else:
                    above = rs(above, -2)
                return sums_of(
                    u, jnp.where(m0, above, rs(u[3], 1)), jnp.where(m3, below, rs(u[0], -1))
                )
            return sa

        carry = begin(sa_of(0), 0)
        carry = along(0, 32, sa_of(0), finalize, carry, unroll)
        along(32, 32, sa_of(1), finalize, carry, unroll)

    def halo_stage(u_at, local_at, finalize, unroll=4):
        def sa(j):
            u = u_at(j + 1)
            up0 = jnp.where(m3, local_at(j + 33, 3), rs(local_at(j + 1, 3), -2))
            down3 = jnp.where(m0, local_at(j + 1, 0), rs(local_at(j + 33, 0), 2))
            return sums_of(u, up0, down3)

        along(0, 32, sa, finalize, begin(sa, 0), unroll)

    def pad_halo(ref):
        for t in range(4):
            ref[0, t] = jnp.where(half0, 0.0, rs(ref[32, t], 2))
            ref[33, t] = jnp.where(half0, rs(ref[1, t], -2), 0.0)

    def tile_of(ref, n, t):
        return ref[n, pl.ds(t, 8, stride=4), :]

    fine_lane = lax.broadcasted_iota(jnp.int32, (512, 128), 0)
    coarse_lane = lax.broadcasted_iota(jnp.int32, (512, 128), 1)
    squeeze = jnp.where(fine_lane // 4 == coarse_lane, 1.0, 0.0).astype(BF16)
    fine_lane2 = lax.broadcasted_iota(jnp.int32, (128, 512), 1)
    coarse_lane2 = lax.broadcasted_iota(jnp.int32, (128, 512), 0)
    stretch = jnp.where(fine_lane2 // 4 == coarse_lane2, 1.0, 0.0).astype(BF16)

    def exact_dot(x, y):
        high = x.astype(BF16)
        rest = x - high.astype(F32)
        middle = rest.astype(BF16)
        low_part = (rest - middle.astype(F32)).astype(BF16)
        out = jnp.dot(high, y, preferred_element_type=F32)
        out = out + jnp.dot(middle, y, preferred_element_type=F32)
        return out + jnp.dot(low_part, y, preferred_element_type=F32)

    for copy in k_loads:
        copy.wait()

    def speed_body(q, _):
        for i in range(4):
            tiles = [tile_of(KN, 4 * q + i + 1, t) for t in range(4)]
            for t in range(4):
                KL[4 * q + i + 1, t] = tiles[t]
            RS[pl.ds(pl.multiple_of(q * 8, 8), 8), pl.ds(128 * i, 128)] = (tiles[0] + tiles[1]) + (tiles[2] + tiles[3])
        return 0

    lax.fori_loop(0, 16, speed_body, 0)
    CK[pl.ds(1, 16)] = (exact_dot(RS[...][:128], squeeze) * 0.0625).reshape(16, 8, 128)

    for copy in b_loads:
        copy.wait()
    recv_all(k_next, has_prev)
    recv_all(k_prev, has_next)

    def halo_speed(q, _):
        for i in range(4):
            tiles = [tile_of(KHN, 4 * q + i + 1, t) for t in range(4)]
            for t in range(4):
                KH[4 * q + i + 1, t] = tiles[t]
            RS[pl.ds(pl.multiple_of(q * 8, 8), 8), pl.ds(128 * i, 128)] = (tiles[0] + tiles[1]) + (tiles[2] + tiles[3])
        return 0

    lax.fori_loop(0, 8, halo_speed, 0)
    pad_halo(KH)
    ckh = (exact_dot(RS[pl.ds(0, 64), :], squeeze) * 0.0625).reshape(8, 8, 128)

    def coarse_sa(q):
        c = CK[q + 1]
        h = ckh[q % 8]
        if q < 8:
            above, below = h, rs(h, 2)
        else:
            above, below = rs(h, -2), h
        s = jnp.where(m0, above, rs(c, 1)) + jnp.where(m3, below, rs(c, -1))
        return s, c + 0.5 * s

    pairs = [coarse_sa(q) for q in range(16)]
    for q in range(16):
        c = CK[q + 1]
        left = rl(pairs[q][1], 1)
        left = jnp.where(lane0, rl(pairs[q - 1][1], 1) if q else 0.0, left)
        right = rl(pairs[q][1], -1)
        right = jnp.where(lane127, rl(pairs[q + 1][1], -1) if q < 15 else 0.0, right)
        near = pairs[q][0] + left + right
        land_q = jnp.where(lane < 64, land(row_tile, 4 * q), land(row_tile, 4 * q + 2))
        g = c * land_q / (16.0 + 32.0 * c * near)
        GQ[q] = g
        QC[2, q] = 25.6 * c * g
        ICK[q] = 1.0 / c
    for q in range(8):
        ICK[16 + q] = 1.0 / jnp.maximum(ckh[q], 1e-30)

    def coarse_copies(ref, send, recv):
        out = []
        for n, (step, there, back) in enumerate(
            ((1, has_next, has_prev), (-1, has_prev, has_next), (2, has_next2, has_prev2), (-2, has_prev2, has_next2))
        ):
            out.append((pltpu.make_async_remote_copy(
                src_ref=ref.at[2], dst_ref=ref.at[2 - step],
                send_sem=send.at[n], recv_sem=recv.at[n],
                device_id={"tiles": me + step}, device_id_type=MESH), there, back))
        return out

    q_copies = coarse_copies(QC, q_send, q_recv)
    p_copies = coarse_copies(PC, p_send, p_recv)
    for copy, there, _ in q_copies:
        start_all([copy], there)

    def fine_a(j, i, near):
        scale = 0.8 * land(row_tile, j)
        for t in range(4):
            k8 = 8.0 * KL[j + 1, t]
            dg = 1.0 + k8 * near[t]
            r = scale / dg
            DG[j, t] = dg
            CL[j + 1, t] = tile_of(BN, j, t) * r
            WL[j, t] = k8 * r

    local_stage(lambda n: [KL[n, t] for t in range(4)], lambda n, t: KH[n, t], fine_a)

    recv_all(b_next, has_prev)
    recv_all(b_prev, has_next)

    def halo_a(j, i, near):
        scale = jnp.where(
            side0,
            jnp.where(half0, land(prev_tile, j), land(prev_tile, j + 32)),
            jnp.where(half0, land(next_tile, j), land(next_tile, j + 32)),
        ) * 0.8
        for t in range(4):
            k8 = 8.0 * KH[j + 1, t]
            r = scale / (1.0 + k8 * near[t])
            CH[j + 1, t] = tile_of(BHN, j, t) * r
            WH[j, t] = k8 * r

    halo_stage(lambda n: [KH[n, t] for t in range(4)], lambda n, t: KL[n, t], halo_a)
    pad_halo(CH)

    MS[1] = mass_total(0)
    mass_start(1)

    def fine_b(j, i, near):
        for t in range(4):
            FL[j + 1, t] = 1.2 * CL[j + 1, t] + WL[j, t] * near[t]

    def halo_b(j, i, near):
        for t in range(4):
            FH[j + 1, t] = 1.2 * CH[j + 1, t] + WH[j, t] * near[t]

    def product(k, f):
        return lambda n: [k[n, t] * f[n, t] for t in range(4)]

    def product1(k, f):
        return lambda n, t: k[n, t] * f[n, t]

    local_stage(product(KL, CL), product1(KH, CH), fine_b)
    halo_stage(product(KH, CH), product1(KL, CL), halo_b)
    pad_halo(FH)

    def fine_c(j, i, near):
        parts = [
            (CL[j + 1, t] - 0.8 * FL[j + 1, t] + WL[j, t] * near[t]) * DG[j, t] for t in range(4)
        ]
        RS[pl.ds(pl.multiple_of((j // 4) * 8, 8), 8), pl.ds(128 * i, 128)] = (parts[0] + parts[1]) + (parts[2] + parts[3])

    local_stage(product(KL, FL), product1(KH, FH), fine_c)
    PC[2] = exact_dot(RS[...], squeeze).reshape(16, 8, 128) * GQ[...]
    for copy, there, _ in p_copies:
        start_all([copy], there)

    MS[2] = mass_total(1)
    mass_start(2)

    for copy, _, back in q_copies + p_copies:
        recv_all([copy], back)

    for slot in range(5):
        UC[pl.ds(1, 16), slot] = PC[slot]

    def coarse_sweep(old, new, slots):
        def sa(q):
            u = {slot: old[q + 1, slot] for slot in slots}
            s = []
            for slot in slots:
                up, down = rs(u[slot], 1), rs(u[slot], -1)
                if slot - 1 in u:
                    up = jnp.where(m0, rs(u[slot - 1], -3), up)
                if slot + 1 in u:
                    down = jnp.where(m3, rs(u[slot + 1], 3), down)
                s.append(up + down)
            return s, [u[slot] + 0.5 * x for slot, x in zip(slots, s)]

        def finalize(q, i, near):
            for n, slot in enumerate(slots):
                new[q + 1, slot] = 0.2 * old[q + 1, slot] + PC[slot, q] + QC[slot, q] * near[n]

        along(0, 16, sa, finalize, begin(sa, 0), 2)

    wide = range(5)
    narrow = range(1, 4)
    coarse_sweep(UC, UP, wide)
    coarse_sweep(UP, UC, wide)
    coarse_sweep(UC, UP, wide)
    coarse_sweep(UP, UC, wide)
    coarse_sweep(UC, UP, narrow)
    coarse_sweep(UP, UC, narrow)
    coarse_sweep(UC, UP, narrow)

    own = UP[pl.ds(1, 16), 2] * ICK[pl.ds(0, 16)]
    beside = []
    for q in range(8):
        above0, below0 = UP[q + 1, 1], UP[q + 1, 3]
        above1, below1 = UP[q + 9, 1], UP[q + 9, 3]
        rows = jnp.where(
            half0,
            jnp.where(side0, rs(above0, -3), rs(below0, 1)),
            jnp.where(side0, rs(above1, -1), rs(below1, 3)),
        )
        beside.append(rows * ICK[16 + q])
    OH_up = exact_dot(own.reshape(128, 128), stretch)
    RS[...] = OH_up
    OH_side = exact_dot(jnp.concatenate(beside, axis=0), stretch)

    def add_local(q, _):
        for i in range(4):
            up = RS[pl.ds(pl.multiple_of(q * 8, 8), 8), pl.ds(128 * i, 128)]
            for t in range(4):
                FL[4 * q + i + 1, t] = FL[4 * q + i + 1, t] + up
        return 0

    lax.fori_loop(0, 16, add_local, 0)
    RS[pl.ds(0, 64), :] = OH_side

    def add_halo(q, _):
        for i in range(4):
            up = RS[pl.ds(pl.multiple_of(q * 8, 8), 8), pl.ds(128 * i, 128)]
            for t in range(4):
                FH[4 * q + i + 1, t] = FH[4 * q + i + 1, t] + up
        return 0

    lax.fori_loop(0, 8, add_halo, 0)
    pad_halo(FH)

    def fine_d(j, i, near):
        for t in range(4):
            GL[j + 1, t] = 0.2 * FL[j + 1, t] + CL[j + 1, t] + WL[j, t] * near[t]

    def halo_d(j, i, near):
        for t in (0, 3):
            GH[j + 1, t] = 0.2 * FH[j + 1, t] + CH[j + 1, t] + WH[j, t] * near[t]

    local_stage(product(KL, FL), product1(KH, FH), fine_d)
    halo_stage(product(KH, FH), product1(KL, FL), halo_d)
    for t in (0, 3):
        GH[0, t] = jnp.where(half0, 0.0, rs(GH[32, t], 2))
        GH[33, t] = jnp.where(half0, rs(GH[1, t], -2), 0.0)

    mass = jnp.sum(mass_total(2))
    cells = float(2 * 16 * 8192) * ntiles * ncls
    ratio = jnp.where(sub < 4, target_ref[0], target_ref[1]) * cells / jnp.full((8, 128), mass, F32)

    def fine_e(j, i, near):
        level = ratio * land(row_tile, j)
        for t in range(4):
            f = 0.2 * GL[j + 1, t] + CL[j + 1, t] + WL[j, t] * near[t]
            OH[j, pl.ds(t, 8, stride=4), :] = f
            OF[j, pl.ds(t, 8, stride=4), :] = tile_of(SN, j, t) * level / jnp.maximum(f, FLOOR_LEVEL)

    local_stage(product(KL, GL), product1(KH, GH), fine_e)

    outs = []
    for n, (vmem, hbm) in enumerate(((OH, heat_out), (OF, flow_out))):
        for c in range(2):
            for rt in range(2):
                outs.append(pltpu.make_async_copy(
                    vmem.at[:, pl.ds(16 * c + 8 * rt, 8), :], hbm.at[c, rt], sem_out.at[4 * n + 2 * c + rt]))
    for copy in outs:
        copy.start()

    sent_all(k_next + b_next, has_next)
    sent_all(k_prev + b_prev, has_prev)
    for copy, there, _ in q_copies + p_copies:
        sent_all([copy], there)
    for stage in range(3):
        for r in range(1, sizes[stage]):
            mass_copy(stage, r).wait_send()
    for copy in outs:
        copy.wait()


def solution(mesh):
    ntiles, ncls = mesh.shape["tiles"], mesh.shape["cls"]

    def tiles_view(x):
        return x.reshape(2, 2, 8, 64, 128).transpose(0, 1, 3, 2, 4)

    def rows_view(x):
        return x.transpose(0, 1, 3, 2, 4).reshape(2, 16, 8192)

    def on_device(scaling, source, speed, tile_mask, target):
        def body(*refs):
            kernel(ntiles, ncls, *refs)

        def vmem(*shape):
            return pltpu.VMEM(shape, F32)

        dma = pltpu.SemaphoreType.DMA
        any_space = pl.BlockSpec(memory_space=pl.ANY)
        smem = pl.BlockSpec(memory_space=pltpu.SMEM)
        heat, flow = pl.pallas_call(
            body,
            out_shape=[jax.ShapeDtypeStruct((2, 2, 64, 8, 128), F32)] * 2,
            in_specs=[smem, smem, any_space, any_space, any_space],
            out_specs=[any_space, any_space],
            scratch_shapes=[
                vmem(66, 32, 128), vmem(64, 32, 128), vmem(64, 32, 128),
                vmem(34, 32, 128), vmem(32, 32, 128),
                vmem(66, 4, 8, 128), vmem(66, 4, 8, 128), vmem(64, 4, 8, 128), vmem(64, 4, 8, 128),
                vmem(66, 4, 8, 128), vmem(66, 4, 8, 128),
                vmem(34, 4, 8, 128), vmem(34, 4, 8, 128), vmem(32, 4, 8, 128),
                vmem(34, 4, 8, 128), vmem(34, 4, 8, 128),
                vmem(128, 512),
                vmem(18, 8, 128), vmem(16, 8, 128), vmem(24, 8, 128),
                vmem(5, 16, 8, 128), vmem(5, 16, 8, 128),
                vmem(18, 5, 8, 128), vmem(18, 5, 8, 128),
                vmem(64, 32, 128), vmem(64, 32, 128),
                vmem(3, 8, 128), vmem(20, 8, 128),
                dma((12,)), dma((8,)),
                dma((8,)), dma((8,)), dma((8,)), dma((8,)),
                dma((4,)), dma((4,)), dma((4,)), dma((4,)),
                dma((20,)), dma((20,)),
            ],
            compiler_params=pltpu.CompilerParams(
                collective_id=0, has_side_effects=True, vmem_limit_bytes=48 * 2**20
            ),
        )(tile_mask, target, tiles_view(scaling), tiles_view(source), tiles_view(speed))
        return rows_view(heat), rows_view(flow)

    placed = (P("cls", "tiles", None), P("cls", "tiles", None), P("cls", "tiles", None), P(), P("cls"))
    return jax.shard_map(
        on_device,
        mesh=mesh,
        in_specs=placed,
        out_specs=(P("cls", "tiles", None), P("cls", "tiles", None)),
        check_vma=False,
    )
```

```python
import jax
import jax.numpy as jnp
from jax import lax
from jax.experimental import pallas as pl
from jax.experimental.pallas import tpu as pltpu
from jax.sharding import PartitionSpec as P

MESH = pl.DeviceIdType.MESH
F32 = jnp.float32
BF16 = jnp.bfloat16
FLOOR_LEVEL = 0.25
TS = 256


def kernel(
    ntiles, ncls,
    mask_ref, target_ref, b_in, src_in, k_in,
    heat_out, flow_out,
    KN, BN, SN, KHN, BHN, KL, CL, WL, DG, FL, GL, KH, CH, WH, FH, GH, RS, CK, GQ, ICK, PC, QC, UC, UP, OH, OF, MS, MR,
    sem_in, sem_out, k_send, k_recv, b_send, b_recv, q_send, q_recv, p_send, p_recv, m_send, m_recv,
):
    me = lax.axis_index("tiles")
    cl = lax.axis_index("cls")
    has_prev, has_next = me > 0, me < ntiles - 1
    has_prev2, has_next2 = me > 1, me < ntiles - 2

    sub = lax.broadcasted_iota(jnp.int32, (8, 128), 0)
    lane = lax.broadcasted_iota(jnp.int32, (8, 128), 1)
    s4 = sub & 3
    m0, m3 = s4 == 0, s4 == 3
    half0 = s4 < 2
    side0 = (sub & 1) == 0
    lane0, lane127 = lane == 0, lane == 127
    zero = jnp.zeros((8, 128), F32)

    def rs(x, n):
        return pltpu.roll(x, n % 8, 0)

    def rl(x, n):
        return pltpu.roll(x, n % 128, 1)

    def load_copies(hbm, vmem, base, s):
        return [
            pltpu.make_async_copy(
                hbm.at[c, rt], vmem.at[pl.ds(base, 64), pl.ds(16 * c + 8 * rt, 8), :], sem_in.at[s * 4 + 2 * c + rt]
            )
            for c in range(2)
            for rt in range(2)
        ]

    k_loads = load_copies(k_in, KN, 1, 0)
    b_loads = load_copies(b_in, BN, 0, 1)
    s_loads = load_copies(src_in, SN, 0, 2)
    for copy in k_loads + s_loads + b_loads:
        copy.start()

    low = me % 8
    mid = me // 8 % 2
    high = me // 16
    place = 2 * mid + cl

    def mass_peer(stage, r):
        if stage == 0:
            return {"tiles": me - low + (low + r) % 8, "cls": cl}
        if stage == 1:
            other = (place + r) % 4
            return {"tiles": me + 8 * (other // 2 - mid), "cls": other % 2}
        return {"tiles": me + 16 * ((high + r) % 8 - high), "cls": cl}

    sizes = (8, 4, 8)
    starts = (0, 8, 12)

    barrier = pltpu.get_barrier_semaphore()

    def greet(there):
        pl.semaphore_signal(barrier, inc=1, device_id=there, device_id_type=MESH)

    for step, there in ((-1, has_prev), (1, has_next), (-2, has_prev2), (2, has_next2)):
        @pl.when(there)
        def _():
            greet({"tiles": me + step})
    for stage in range(3):
        for r in range(1, sizes[stage]):
            greet(mass_peer(stage, r))
    one = jnp.int32(1)
    nil = jnp.int32(0)
    greeted = 17
    for there in (has_prev, has_next, has_prev2, has_next2):
        greeted = greeted + jnp.where(there, one, nil)
    pl.semaphore_wait(barrier, greeted)

    def halo_copies(hbm, vmem, base, send, recv):
        to_next, to_prev = [], []
        for c in range(2):
            for half in range(2):
                n = 2 * c + half
                to_next.append(pltpu.make_async_remote_copy(
                    src_ref=hbm.at[c, 1, pl.ds(32 * half, 32), pl.ds(4, 4), :],
                    dst_ref=vmem.at[pl.ds(base, 32), pl.ds(16 * c + 8 * half, 4), :],
                    send_sem=send.at[n], recv_sem=recv.at[n],
                    device_id={"tiles": me + 1}, device_id_type=MESH))
                to_prev.append(pltpu.make_async_remote_copy(
                    src_ref=hbm.at[c, 0, pl.ds(32 * half, 32), pl.ds(0, 4), :],
                    dst_ref=vmem.at[pl.ds(base, 32), pl.ds(16 * c + 8 * half + 4, 4), :],
                    send_sem=send.at[4 + n], recv_sem=recv.at[4 + n],
                    device_id={"tiles": me - 1}, device_id_type=MESH))
        return to_next, to_prev

    k_next, k_prev = halo_copies(k_in, KHN, 1, k_send, k_recv)
    b_next, b_prev = halo_copies(b_in, BHN, 0, b_send, b_recv)

    def start_all(copies, there):
        @pl.when(there)
        def _():
            for copy in copies:
                copy.start()

    def recv_all(copies, there):
        @pl.when(there)
        def _():
            for copy in copies:
                copy.wait_recv()

    def sent_all(copies, there):
        @pl.when(there)
        def _():
            for copy in copies:
                copy.wait_send()

    start_all(k_next, has_next)
    start_all(k_prev, has_prev)
    start_all(b_next, has_next)
    start_all(b_prev, has_prev)

    for n in (0, 65):
        KN[n] = jnp.zeros((32, 128), F32)
        for t in range(4):
            KL[n, t] = zero
            CL[n, t] = zero
            FL[n, t] = zero
            GL[n, t] = zero

    def outside(first, there):
        @pl.when(jnp.logical_not(there))
        def _():
            for c in range(2):
                for half in range(2):
                    row = 16 * c + 8 * half + first
                    KHN[pl.ds(1, 32), pl.ds(row, 4), :] = jnp.zeros((32, 4, 128), F32)
                    BHN[pl.ds(0, 32), pl.ds(row, 4), :] = jnp.zeros((32, 4, 128), F32)

    outside(0, has_prev)
    outside(4, has_next)

    def clear(slot, there):
        @pl.when(jnp.logical_not(there))
        def _():
            PC[slot] = jnp.zeros((16, 8, 128), F32)
            QC[slot] = jnp.zeros((16, 8, 128), F32)

    clear(0, has_prev2)
    clear(1, has_prev)
    clear(3, has_next)
    clear(4, has_next2)
    for q in (0, 17):
        for slot in range(5):
            UC[q, slot] = zero
            UP[q, slot] = zero
        CK[q] = zero

    def mass_copy(stage, r):
        return pltpu.make_async_remote_copy(
            src_ref=MS.at[stage], dst_ref=MR.at[starts[stage] + r],
            send_sem=m_send.at[starts[stage] + r], recv_sem=m_recv.at[starts[stage] + r],
            device_id=mass_peer(stage, r), device_id_type=MESH)

    def mass_start(stage):
        for r in range(1, sizes[stage]):
            mass_copy(stage, r).start()

    def mass_total(stage):
        total = MS[stage]
        for r in range(1, sizes[stage]):
            mass_copy(stage, r).wait_recv()
        for r in range(1, sizes[stage]):
            total = total + MR[starts[stage] + r]
        return total

    for copy in s_loads:
        copy.wait()

    def add_source(n, sums):
        return tuple(
            sums[i] + SN[n * 2 + i // 4, pl.ds(8 * (i % 4), 8), :] for i in range(8)
        )

    sums = lax.fori_loop(0, 32, add_source, (zero,) * 8)
    total = sums[0]
    for part in sums[1:]:
        total = total + part
    MS[0] = total
    mass_start(0)

    row_tile = me * 16 // TS
    prev_tile = jnp.maximum(me * 16 - 1, 0) // TS
    next_tile = jnp.minimum(me * 16 + 16, ntiles * 16 - 1) // TS

    def land(row, block):
        return mask_ref[row, block // 2].astype(F32)

    def along(first, count, sa, finalize, carry, unroll):
        def body(n, carry):
            for i in range(unroll):
                j = first + n * unroll + i
                before, s, right, left = carry
                s_next, a_next = sa(j + 1)
                right_next = [rl(x, 1) for x in a_next]
                left_next = [rl(x, -1) for x in a_next]
                near = [
                    s[t] + jnp.where(lane0, before[t], right[t]) + jnp.where(lane127, left_next[t], left[t])
                    for t in range(len(s))
                ]
                finalize(j, i, near)
                carry = (right, s_next, right_next, left_next)
            return carry

        return lax.fori_loop(0, count // unroll, body, carry)

    def begin(sa, first):
        _, a_before = sa(first - 1)
        s, a = sa(first)
        return ([rl(x, 1) for x in a_before], s, [rl(x, 1) for x in a], [rl(x, -1) for x in a])

    def sums_of(u, up0, down3):
        s = [up0 + u[1], u[0] + u[2], u[1] + u[3], u[2] + down3]
        return s, [u[t] + 0.5 * s[t] for t in range(4)]

    def local_stage(u_at, edge_at, finalize, unroll=32):
        def sa_of(half):
            def sa(j):
                u = u_at(j + 1)
                h = j - 32 * half + 1
                above, below = edge_at(h, 3), edge_at(h, 0)
                if half == 0:
                    below = rs(below, 2)
                else:
                    above = rs(above, -2)
                return sums_of(
                    u, jnp.where(m0, above, rs(u[3], 1)), jnp.where(m3, below, rs(u[0], -1))
                )
            return sa

        carry = begin(sa_of(0), 0)
        carry = along(0, 32, sa_of(0), finalize, carry, unroll)
        along(32, 32, sa_of(1), finalize, carry, unroll)

    def halo_stage(u_at, local_at, finalize, unroll=32):
        def sa(j):
            u = u_at(j + 1)
            up0 = jnp.where(m3, local_at(j + 33, 3), rs(local_at(j + 1, 3), -2))
            down3 = jnp.where(m0, local_at(j + 1, 0), rs(local_at(j + 33, 0), 2))
            return sums_of(u, up0, down3)

        along(0, 32, sa, finalize, begin(sa, 0), unroll)

    def pad_halo(ref):
        for t in range(4):
            ref[0, t] = jnp.where(half0, 0.0, rs(ref[32, t], 2))
            ref[33, t] = jnp.where(half0, rs(ref[1, t], -2), 0.0)

    def tile_of(ref, n, t):
        return ref[n, pl.ds(t, 8, stride=4), :]

    fine_lane = lax.broadcasted_iota(jnp.int32, (512, 128), 0)
    coarse_lane = lax.broadcasted_iota(jnp.int32, (512, 128), 1)
    squeeze = jnp.where(fine_lane // 4 == coarse_lane, 1.0, 0.0).astype(BF16)
    fine_lane2 = lax.broadcasted_iota(jnp.int32, (128, 512), 1)
    coarse_lane2 = lax.broadcasted_iota(jnp.int32, (128, 512), 0)
    stretch = jnp.where(fine_lane2 // 4 == coarse_lane2, 1.0, 0.0).astype(BF16)

    def exact_dot(x, y):
        high = x.astype(BF16)
        rest = x - high.astype(F32)
        middle = rest.astype(BF16)
        low_part = (rest - middle.astype(F32)).astype(BF16)
        out = jnp.dot(high, y, preferred_element_type=F32)
        out = out + jnp.dot(middle, y, preferred_element_type=F32)
        return out + jnp.dot(low_part, y, preferred_element_type=F32)

    for copy in k_loads:
        copy.wait()

    def speed_body(q, _):
        for i in range(4):
            tiles = [tile_of(KN, 4 * q + i + 1, t) for t in range(4)]
            for t in range(4):
                KL[4 * q + i + 1, t] = tiles[t]
            RS[pl.ds(pl.multiple_of(q * 8, 8), 8), pl.ds(128 * i, 128)] = (tiles[0] + tiles[1]) + (tiles[2] + tiles[3])
        return 0

    lax.fori_loop(0, 16, speed_body, 0)
    CK[pl.ds(1, 16)] = (exact_dot(RS[...][:128], squeeze) * 0.0625).reshape(16, 8, 128)

    for copy in b_loads:
        copy.wait()
    recv_all(k_next, has_prev)
    recv_all(k_prev, has_next)

    def halo_speed(q, _):
        for i in range(4):
            tiles = [tile_of(KHN, 4 * q + i + 1, t) for t in range(4)]
            for t in range(4):
                KH[4 * q + i + 1, t] = tiles[t]
            RS[pl.ds(pl.multiple_of(q * 8, 8), 8), pl.ds(128 * i, 128)] = (tiles[0] + tiles[1]) + (tiles[2] + tiles[3])
        return 0

    lax.fori_loop(0, 8, halo_speed, 0)
    pad_halo(KH)
    ckh = (exact_dot(RS[pl.ds(0, 64), :], squeeze) * 0.0625).reshape(8, 8, 128)

    def coarse_sa(q):
        c = CK[q + 1]
        h = ckh[q % 8]
        if q < 8:
            above, below = h, rs(h, 2)
        else:
            above, below = rs(h, -2), h
        s = jnp.where(m0, above, rs(c, 1)) + jnp.where(m3, below, rs(c, -1))
        return s, c + 0.5 * s

    pairs = [coarse_sa(q) for q in range(16)]
    for q in range(16):
        c = CK[q + 1]
        left = rl(pairs[q][1], 1)
        left = jnp.where(lane0, rl(pairs[q - 1][1], 1) if q else 0.0, left)
        right = rl(pairs[q][1], -1)
        right = jnp.where(lane127, rl(pairs[q + 1][1], -1) if q < 15 else 0.0, right)
        near = pairs[q][0] + left + right
        land_q = jnp.where(lane < 64, land(row_tile, 4 * q), land(row_tile, 4 * q + 2))
        g = c * land_q / (16.0 + 32.0 * c * near)
        GQ[q] = g
        QC[2, q] = 25.6 * c * g
        ICK[q] = 1.0 / c
    for q in range(8):
        ICK[16 + q] = 1.0 / jnp.maximum(ckh[q], 1e-30)

    def coarse_copies(ref, send, recv):
        out = []
        for n, (step, there, back) in enumerate(
            ((1, has_next, has_prev), (-1, has_prev, has_next), (2, has_next2, has_prev2), (-2, has_prev2, has_next2))
        ):
            out.append((pltpu.make_async_remote_copy(
                src_ref=ref.at[2], dst_ref=ref.at[2 - step],
                send_sem=send.at[n], recv_sem=recv.at[n],
                device_id={"tiles": me + step}, device_id_type=MESH), there, back))
        return out

    q_copies = coarse_copies(QC, q_send, q_recv)
    p_copies = coarse_copies(PC, p_send, p_recv)
    for copy, there, _ in q_copies:
        start_all([copy], there)

    def fine_a(j, i, near):
        scale = 0.8 * land(row_tile, j)
        for t in range(4):
            k8 = 8.0 * KL[j + 1, t]
            dg = 1.0 + k8 * near[t]
            r = scale / dg
            DG[j, t] = dg
            CL[j + 1, t] = tile_of(BN, j, t) * r
            WL[j, t] = k8 * r

    local_stage(lambda n: [KL[n, t] for t in range(4)], lambda n, t: KH[n, t], fine_a)

    recv_all(b_next, has_prev)
    recv_all(b_prev, has_next)

    def halo_a(j, i, near):
        scale = jnp.where(
            side0,
            jnp.where(half0, land(prev_tile, j), land(prev_tile, j + 32)),
            jnp.where(half0, land(next_tile, j), land(next_tile, j + 32)),
        ) * 0.8
        for t in range(4):
            k8 = 8.0 * KH[j + 1, t]
            r = scale / (1.0 + k8 * near[t])
            CH[j + 1, t] = tile_of(BHN, j, t) * r
            WH[j, t] = k8 * r

    halo_stage(lambda n: [KH[n, t] for t in range(4)], lambda n, t: KL[n, t], halo_a)
    pad_halo(CH)

    MS[1] = mass_total(0)
    mass_start(1)

    def fine_b(j, i, near):
        for t in range(4):
            FL[j + 1, t] = 1.2 * CL[j + 1, t] + WL[j, t] * near[t]

    def halo_b(j, i, near):
        for t in range(4):
            FH[j + 1, t] = 1.2 * CH[j + 1, t] + WH[j, t] * near[t]

    def product(k, f):
        return lambda n: [k[n, t] * f[n, t] for t in range(4)]

    def product1(k, f):
        return lambda n, t: k[n, t] * f[n, t]

    local_stage(product(KL, CL), product1(KH, CH), fine_b)
    halo_stage(product(KH, CH), product1(KL, CL), halo_b)
    pad_halo(FH)

    def fine_c(j, i, near):
        parts = [
            (CL[j + 1, t] - 0.8 * FL[j + 1, t] + WL[j, t] * near[t]) * DG[j, t] for t in range(4)
        ]
        RS[pl.ds(pl.multiple_of((j // 4) * 8, 8), 8), pl.ds(128 * (i % 4), 128)] = (parts[0] + parts[1]) + (parts[2] + parts[3])

    local_stage(product(KL, FL), product1(KH, FH), fine_c)
    PC[2] = exact_dot(RS[...], squeeze).reshape(16, 8, 128) * GQ[...]
    for copy, there, _ in p_copies:
        start_all([copy], there)

    MS[2] = mass_total(1)
    mass_start(2)

    for copy, _, back in q_copies + p_copies:
        recv_all([copy], back)

    for slot in range(5):
        UC[pl.ds(1, 16), slot] = PC[slot]

    def coarse_sweep(old, new, slots):
        def sa(q):
            u = {slot: old[q + 1, slot] for slot in slots}
            s = []
            for slot in slots:
                up, down = rs(u[slot], 1), rs(u[slot], -1)
                if slot - 1 in u:
                    up = jnp.where(m0, rs(u[slot - 1], -3), up)
                if slot + 1 in u:
                    down = jnp.where(m3, rs(u[slot + 1], 3), down)
                s.append(up + down)
            return s, [u[slot] + 0.5 * x for slot, x in zip(slots, s)]

        def finalize(q, i, near):
            for n, slot in enumerate(slots):
                new[q + 1, slot] = 0.2 * old[q + 1, slot] + PC[slot, q] + QC[slot, q] * near[n]

        along(0, 16, sa, finalize, begin(sa, 0), 16)

    wide = range(5)
    narrow = range(1, 4)
    coarse_sweep(UC, UP, wide)
    coarse_sweep(UP, UC, wide)
    coarse_sweep(UC, UP, wide)
    coarse_sweep(UP, UC, wide)
    coarse_sweep(UC, UP, narrow)
    coarse_sweep(UP, UC, narrow)
    coarse_sweep(UC, UP, narrow)

    own = UP[pl.ds(1, 16), 2] * ICK[pl.ds(0, 16)]
    beside = []
    for q in range(8):
        above0, below0 = UP[q + 1, 1], UP[q + 1, 3]
        above1, below1 = UP[q + 9, 1], UP[q + 9, 3]
        rows = jnp.where(
            half0,
            jnp.where(side0, rs(above0, -3), rs(below0, 1)),
            jnp.where(side0, rs(above1, -1), rs(below1, 3)),
        )
        beside.append(rows * ICK[16 + q])
    OH_up = exact_dot(own.reshape(128, 128), stretch)
    RS[...] = OH_up
    OH_side = exact_dot(jnp.concatenate(beside, axis=0), stretch)

    def add_local(q, _):
        for i in range(4):
            up = RS[pl.ds(pl.multiple_of(q * 8, 8), 8), pl.ds(128 * i, 128)]
            for t in range(4):
                FL[4 * q + i + 1, t] = FL[4 * q + i + 1, t] + up
        return 0

    lax.fori_loop(0, 16, add_local, 0)
    RS[pl.ds(0, 64), :] = OH_side

    def add_halo(q, _):
        for i in range(4):
            up = RS[pl.ds(pl.multiple_of(q * 8, 8), 8), pl.ds(128 * i, 128)]
            for t in range(4):
                FH[4 * q + i + 1, t] = FH[4 * q + i + 1, t] + up
        return 0

    lax.fori_loop(0, 8, add_halo, 0)
    pad_halo(FH)

    def fine_d(j, i, near):
        for t in range(4):
            GL[j + 1, t] = 0.2 * FL[j + 1, t] + CL[j + 1, t] + WL[j, t] * near[t]

    def halo_d(j, i, near):
        for t in (0, 3):
            GH[j + 1, t] = 0.2 * FH[j + 1, t] + CH[j + 1, t] + WH[j, t] * near[t]

    local_stage(product(KL, FL), product1(KH, FH), fine_d)
    halo_stage(product(KH, FH), product1(KL, FL), halo_d)
    for t in (0, 3):
        GH[0, t] = jnp.where(half0, 0.0, rs(GH[32, t], 2))
        GH[33, t] = jnp.where(half0, rs(GH[1, t], -2), 0.0)

    mass = jnp.sum(mass_total(2))
    cells = float(2 * 16 * 8192) * ntiles * ncls
    ratio = jnp.where(sub < 4, target_ref[0], target_ref[1]) * cells / jnp.full((8, 128), mass, F32)

    def fine_e(j, i, near):
        level = ratio * land(row_tile, j)
        for t in range(4):
            f = 0.2 * GL[j + 1, t] + CL[j + 1, t] + WL[j, t] * near[t]
            OH[j, pl.ds(t, 8, stride=4), :] = f
            OF[j, pl.ds(t, 8, stride=4), :] = tile_of(SN, j, t) * level / jnp.maximum(f, FLOOR_LEVEL)

    local_stage(product(KL, GL), product1(KH, GH), fine_e)

    outs = []
    for n, (vmem, hbm) in enumerate(((OH, heat_out), (OF, flow_out))):
        for c in range(2):
            for rt in range(2):
                outs.append(pltpu.make_async_copy(
                    vmem.at[:, pl.ds(16 * c + 8 * rt, 8), :], hbm.at[c, rt], sem_out.at[4 * n + 2 * c + rt]))
    for copy in outs:
        copy.start()

    sent_all(k_next + b_next, has_next)
    sent_all(k_prev + b_prev, has_prev)
    for copy, there, _ in q_copies + p_copies:
        sent_all([copy], there)
    for stage in range(3):
        for r in range(1, sizes[stage]):
            mass_copy(stage, r).wait_send()
    for copy in outs:
        copy.wait()


def solution(mesh):
    ntiles, ncls = mesh.shape["tiles"], mesh.shape["cls"]

    def tiles_view(x):
        return x.reshape(2, 2, 8, 64, 128).transpose(0, 1, 3, 2, 4)

    def rows_view(x):
        return x.transpose(0, 1, 3, 2, 4).reshape(2, 16, 8192)

    def on_device(scaling, source, speed, tile_mask, target):
        def body(*refs):
            kernel(ntiles, ncls, *refs)

        def vmem(*shape):
            return pltpu.VMEM(shape, F32)

        dma = pltpu.SemaphoreType.DMA
        any_space = pl.BlockSpec(memory_space=pl.ANY)
        smem = pl.BlockSpec(memory_space=pltpu.SMEM)
        heat, flow = pl.pallas_call(
            body,
            out_shape=[jax.ShapeDtypeStruct((2, 2, 64, 8, 128), F32)] * 2,
            in_specs=[smem, smem, any_space, any_space, any_space],
            out_specs=[any_space, any_space],
            scratch_shapes=[
                vmem(66, 32, 128), vmem(64, 32, 128), vmem(64, 32, 128),
                vmem(34, 32, 128), vmem(32, 32, 128),
                vmem(66, 4, 8, 128), vmem(66, 4, 8, 128), vmem(64, 4, 8, 128), vmem(64, 4, 8, 128),
                vmem(66, 4, 8, 128), vmem(66, 4, 8, 128),
                vmem(34, 4, 8, 128), vmem(34, 4, 8, 128), vmem(32, 4, 8, 128),
                vmem(34, 4, 8, 128), vmem(34, 4, 8, 128),
                vmem(128, 512),
                vmem(18, 8, 128), vmem(16, 8, 128), vmem(24, 8, 128),
                vmem(5, 16, 8, 128), vmem(5, 16, 8, 128),
                vmem(18, 5, 8, 128), vmem(18, 5, 8, 128),
                vmem(64, 32, 128), vmem(64, 32, 128),
                vmem(3, 8, 128), vmem(20, 8, 128),
                dma((12,)), dma((8,)),
                dma((8,)), dma((8,)), dma((8,)), dma((8,)),
                dma((4,)), dma((4,)), dma((4,)), dma((4,)),
                dma((20,)), dma((20,)),
            ],
            compiler_params=pltpu.CompilerParams(
                collective_id=0, has_side_effects=True, vmem_limit_bytes=48 * 2**20
            ),
        )(tile_mask, target, tiles_view(scaling), tiles_view(source), tiles_view(speed))
        return rows_view(heat), rows_view(flow)

    placed = (P("cls", "tiles", None), P("cls", "tiles", None), P("cls", "tiles", None), P(), P("cls"))
    return jax.shard_map(
        on_device,
        mesh=mesh,
        in_specs=placed,
        out_specs=(P("cls", "tiles", None), P("cls", "tiles", None)),
        check_vma=False,
    )
```

```python
import jax
import jax.numpy as jnp
from jax import lax
from jax.experimental import pallas as pl
from jax.experimental.pallas import tpu as pltpu
from jax.sharding import PartitionSpec as P

MESH = pl.DeviceIdType.MESH
F32 = jnp.float32
BF16 = jnp.bfloat16
FLOOR_LEVEL = 0.25
TS = 256


def kernel(
    ntiles, ncls,
    mask_in, target_in, b_in, src_in, k_in,
    OH, OF,
    KN, BN, SN, KHN, BHN, KL, CL, WL, DG, FL, GL, KH, CH, WH, FH, GH, RS, CK, GQ, ICK, PC, QC, UC, UP, MS, MR, mask_ref, target_ref,
    sem_in, k_send, k_recv, b_send, b_recv, q_send, q_recv, p_send, p_recv, m_send, m_recv,
):
    me = lax.axis_index("tiles")
    cl = lax.axis_index("cls")
    has_prev, has_next = me > 0, me < ntiles - 1
    has_prev2, has_next2 = me > 1, me < ntiles - 2

    sub = lax.broadcasted_iota(jnp.int32, (8, 128), 0)
    lane = lax.broadcasted_iota(jnp.int32, (8, 128), 1)
    s4 = sub & 3
    m0, m3 = s4 == 0, s4 == 3
    half0 = s4 < 2
    side0 = (sub & 1) == 0
    lane0, lane127 = lane == 0, lane == 127
    zero = jnp.zeros((8, 128), F32)

    def rs(x, n):
        return pltpu.roll(x, n % 8, 0)

    def rl(x, n):
        return pltpu.roll(x, n % 128, 1)

    low = me % 8
    mid = me // 8 % 2
    high = me // 16
    place = 2 * mid + cl

    def mass_peer(stage, r):
        if stage == 0:
            return {"tiles": me - low + (low + r) % 8, "cls": cl}
        if stage == 1:
            other = (place + r) % 4
            return {"tiles": me + 8 * (other // 2 - mid), "cls": other % 2}
        return {"tiles": me + 16 * ((high + r) % 8 - high), "cls": cl}

    sizes = (8, 4, 8)
    starts = (0, 8, 12)

    barrier = pltpu.get_barrier_semaphore()

    def greet(there):
        pl.semaphore_signal(barrier, inc=1, device_id=there, device_id_type=MESH)

    for step, there in ((-1, has_prev), (1, has_next), (-2, has_prev2), (2, has_next2)):
        @pl.when(there)
        def _():
            greet({"tiles": me + step})
    for stage in range(3):
        for r in range(1, sizes[stage]):
            greet(mass_peer(stage, r))
    def load_copies(hbm, vmem, base, s):
        return [
            pltpu.make_async_copy(
                hbm.at[c, rt], vmem.at[pl.ds(base, 64), pl.ds(16 * c + 8 * rt, 8), :], sem_in.at[s * 4 + 2 * c + rt]
            )
            for c in range(2)
            for rt in range(2)
        ]

    k_loads = load_copies(k_in, KN, 1, 0)
    b_loads = load_copies(b_in, BN, 0, 1)
    s_loads = load_copies(src_in, SN, 0, 2)
    small_loads = [
        pltpu.make_async_copy(mask_in, mask_ref, sem_in.at[12]),
        pltpu.make_async_copy(target_in, target_ref, sem_in.at[13]),
    ]
    for copy in k_loads + s_loads + small_loads + b_loads:
        copy.start()

    one = jnp.int32(1)
    nil = jnp.int32(0)
    greeted = 17
    for there in (has_prev, has_next, has_prev2, has_next2):
        greeted = greeted + jnp.where(there, one, nil)
    pl.semaphore_wait(barrier, greeted)

    def halo_copies(hbm, vmem, base, send, recv):
        to_next, to_prev = [], []
        for c in range(2):
            for half in range(2):
                n = 2 * c + half
                to_next.append(pltpu.make_async_remote_copy(
                    src_ref=hbm.at[c, 1, pl.ds(32 * half, 32), pl.ds(4, 4), :],
                    dst_ref=vmem.at[pl.ds(base, 32), pl.ds(16 * c + 8 * half, 4), :],
                    send_sem=send.at[n], recv_sem=recv.at[n],
                    device_id={"tiles": me + 1}, device_id_type=MESH))
                to_prev.append(pltpu.make_async_remote_copy(
                    src_ref=hbm.at[c, 0, pl.ds(32 * half, 32), pl.ds(0, 4), :],
                    dst_ref=vmem.at[pl.ds(base, 32), pl.ds(16 * c + 8 * half + 4, 4), :],
                    send_sem=send.at[4 + n], recv_sem=recv.at[4 + n],
                    device_id={"tiles": me - 1}, device_id_type=MESH))
        return to_next, to_prev

    k_next, k_prev = halo_copies(k_in, KHN, 1, k_send, k_recv)
    b_next, b_prev = halo_copies(b_in, BHN, 0, b_send, b_recv)

    def start_all(copies, there):
        @pl.when(there)
        def _():
            for copy in copies:
                copy.start()

    def recv_all(copies, there):
        @pl.when(there)
        def _():
            for copy in copies:
                copy.wait_recv()

    def sent_all(copies, there):
        @pl.when(there)
        def _():
            for copy in copies:
                copy.wait_send()

    start_all(k_next, has_next)
    start_all(k_prev, has_prev)
    start_all(b_next, has_next)
    start_all(b_prev, has_prev)

    for n in (0, 65):
        KN[n] = jnp.zeros((32, 128), F32)
        for t in range(4):
            KL[n, t] = zero
            CL[n, t] = zero
            FL[n, t] = zero
            GL[n, t] = zero

    def outside(first, there):
        @pl.when(jnp.logical_not(there))
        def _():
            for c in range(2):
                for half in range(2):
                    row = 16 * c + 8 * half + first
                    KHN[pl.ds(1, 32), pl.ds(row, 4), :] = jnp.zeros((32, 4, 128), F32)
                    BHN[pl.ds(0, 32), pl.ds(row, 4), :] = jnp.zeros((32, 4, 128), F32)

    outside(0, has_prev)
    outside(4, has_next)

    def clear(slot, there):
        @pl.when(jnp.logical_not(there))
        def _():
            PC[slot] = jnp.zeros((16, 8, 128), F32)
            QC[slot] = jnp.zeros((16, 8, 128), F32)

    clear(0, has_prev2)
    clear(1, has_prev)
    clear(3, has_next)
    clear(4, has_next2)
    for q in (0, 17):
        for slot in range(5):
            UC[q, slot] = zero
            UP[q, slot] = zero
        CK[q] = zero

    def mass_copy(stage, r):
        return pltpu.make_async_remote_copy(
            src_ref=MS.at[stage], dst_ref=MR.at[starts[stage] + r],
            send_sem=m_send.at[starts[stage] + r], recv_sem=m_recv.at[starts[stage] + r],
            device_id=mass_peer(stage, r), device_id_type=MESH)

    def mass_start(stage):
        for r in range(1, sizes[stage]):
            mass_copy(stage, r).start()

    def mass_total(stage):
        total = MS[stage]
        for r in range(1, sizes[stage]):
            mass_copy(stage, r).wait_recv()
        for r in range(1, sizes[stage]):
            total = total + MR[starts[stage] + r]
        return total

    for copy in s_loads + small_loads:
        copy.wait()

    def add_source(n, sums):
        return tuple(
            sums[i] + SN[n * 2 + i // 4, pl.ds(8 * (i % 4), 8), :] for i in range(8)
        )

    sums = lax.fori_loop(0, 32, add_source, (zero,) * 8)
    total = sums[0]
    for part in sums[1:]:
        total = total + part
    MS[0] = total
    mass_start(0)

    row_tile = me * 16 // TS
    prev_tile = jnp.maximum(me * 16 - 1, 0) // TS
    next_tile = jnp.minimum(me * 16 + 16, ntiles * 16 - 1) // TS

    def land(row, block):
        return mask_ref[row, block // 2].astype(F32)

    def along(first, count, sa, finalize, carry, unroll):
        def body(n, carry):
            for i in range(unroll):
                j = first + n * unroll + i
                before, s, right, left = carry
                s_next, a_next = sa(j + 1)
                right_next = [rl(x, 1) for x in a_next]
                left_next = [rl(x, -1) for x in a_next]
                near = [
                    s[t] + jnp.where(lane0, before[t], right[t]) + jnp.where(lane127, left_next[t], left[t])
                    for t in range(len(s))
                ]
                finalize(j, i, near)
                carry = (right, s_next, right_next, left_next)
            return carry

        return lax.fori_loop(0, count // unroll, body, carry)

    def begin(sa, first):
        _, a_before = sa(first - 1)
        s, a = sa(first)
        return ([rl(x, 1) for x in a_before], s, [rl(x, 1) for x in a], [rl(x, -1) for x in a])

    def sums_of(u, up0, down3):
        s = [up0 + u[1], u[0] + u[2], u[1] + u[3], u[2] + down3]
        return s, [u[t] + 0.5 * s[t] for t in range(4)]

    def local_stage(u_at, edge_at, finalize, unroll=32):
        def sa_of(half):
            def sa(j):
                u = u_at(j + 1)
                h = j - 32 * half + 1
                above, below = edge_at(h, 3), edge_at(h, 0)
                if half == 0:
                    below = rs(below, 2)
                else:
                    above = rs(above, -2)
                return sums_of(
                    u, jnp.where(m0, above, rs(u[3], 1)), jnp.where(m3, below, rs(u[0], -1))
                )
            return sa

        carry = begin(sa_of(0), 0)
        carry = along(0, 32, sa_of(0), finalize, carry, unroll)
        along(32, 32, sa_of(1), finalize, carry, unroll)

    def halo_stage(u_at, local_at, finalize, unroll=32):
        def sa(j):
            u = u_at(j + 1)
            up0 = jnp.where(m3, local_at(j + 33, 3), rs(local_at(j + 1, 3), -2))
            down3 = jnp.where(m0, local_at(j + 1, 0), rs(local_at(j + 33, 0), 2))
            return sums_of(u, up0, down3)

        along(0, 32, sa, finalize, begin(sa, 0), unroll)

    def pad_halo(ref):
        for t in range(4):
            ref[0, t] = jnp.where(half0, 0.0, rs(ref[32, t], 2))
            ref[33, t] = jnp.where(half0, rs(ref[1, t], -2), 0.0)

    def tile_of(ref, n, t):
        return ref[n, pl.ds(t, 8, stride=4), :]

    fine_lane = lax.broadcasted_iota(jnp.int32, (512, 128), 0)
    coarse_lane = lax.broadcasted_iota(jnp.int32, (512, 128), 1)
    squeeze = jnp.where(fine_lane // 4 == coarse_lane, 1.0, 0.0).astype(BF16)
    fine_lane2 = lax.broadcasted_iota(jnp.int32, (128, 512), 1)
    coarse_lane2 = lax.broadcasted_iota(jnp.int32, (128, 512), 0)
    stretch = jnp.where(fine_lane2 // 4 == coarse_lane2, 1.0, 0.0).astype(BF16)

    def exact_dot(x, y):
        high = x.astype(BF16)
        rest = x - high.astype(F32)
        middle = rest.astype(BF16)
        low_part = (rest - middle.astype(F32)).astype(BF16)
        out = jnp.dot(high, y, preferred_element_type=F32)
        out = out + jnp.dot(middle, y, preferred_element_type=F32)
        return out + jnp.dot(low_part, y, preferred_element_type=F32)

    for copy in k_loads:
        copy.wait()

    def speed_body(q, _):
        for i in range(4):
            tiles = [tile_of(KN, 4 * q + i + 1, t) for t in range(4)]
            for t in range(4):
                KL[4 * q + i + 1, t] = tiles[t]
            RS[pl.ds(pl.multiple_of(q * 8, 8), 8), pl.ds(128 * i, 128)] = (tiles[0] + tiles[1]) + (tiles[2] + tiles[3])
        return 0

    lax.fori_loop(0, 16, speed_body, 0)
    CK[pl.ds(1, 16)] = (exact_dot(RS[...][:128], squeeze) * 0.0625).reshape(16, 8, 128)

    for copy in b_loads:
        copy.wait()
    recv_all(k_next, has_prev)
    recv_all(k_prev, has_next)

    def halo_speed(q, _):
        for i in range(4):
            tiles = [tile_of(KHN, 4 * q + i + 1, t) for t in range(4)]
            for t in range(4):
                KH[4 * q + i + 1, t] = tiles[t]
            RS[pl.ds(pl.multiple_of(q * 8, 8), 8), pl.ds(128 * i, 128)] = (tiles[0] + tiles[1]) + (tiles[2] + tiles[3])
        return 0

    lax.fori_loop(0, 8, halo_speed, 0)
    pad_halo(KH)
    ckh = (exact_dot(RS[pl.ds(0, 64), :], squeeze) * 0.0625).reshape(8, 8, 128)

    def coarse_sa(q):
        c = CK[q + 1]
        h = ckh[q % 8]
        if q < 8:
            above, below = h, rs(h, 2)
        else:
            above, below = rs(h, -2), h
        s = jnp.where(m0, above, rs(c, 1)) + jnp.where(m3, below, rs(c, -1))
        return s, c + 0.5 * s

    pairs = [coarse_sa(q) for q in range(16)]
    for q in range(16):
        c = CK[q + 1]
        left = rl(pairs[q][1], 1)
        left = jnp.where(lane0, rl(pairs[q - 1][1], 1) if q else 0.0, left)
        right = rl(pairs[q][1], -1)
        right = jnp.where(lane127, rl(pairs[q + 1][1], -1) if q < 15 else 0.0, right)
        near = pairs[q][0] + left + right
        land_q = jnp.where(lane < 64, land(row_tile, 4 * q), land(row_tile, 4 * q + 2))
        g = c * land_q / (16.0 + 32.0 * c * near)
        GQ[q] = g
        QC[2, q] = 25.6 * c * g
        ICK[q] = 1.0 / c
    for q in range(8):
        ICK[16 + q] = 1.0 / jnp.maximum(ckh[q], 1e-30)

    def coarse_copies(ref, send, recv):
        out = []
        for n, (step, there, back) in enumerate(
            ((1, has_next, has_prev), (-1, has_prev, has_next), (2, has_next2, has_prev2), (-2, has_prev2, has_next2))
        ):
            out.append((pltpu.make_async_remote_copy(
                src_ref=ref.at[2], dst_ref=ref.at[2 - step],
                send_sem=send.at[n], recv_sem=recv.at[n],
                device_id={"tiles": me + step}, device_id_type=MESH), there, back))
        return out

    q_copies = coarse_copies(QC, q_send, q_recv)
    p_copies = coarse_copies(PC, p_send, p_recv)
    for copy, there, _ in q_copies:
        start_all([copy], there)

    def fine_a(j, i, near):
        scale = 0.8 * land(row_tile, j)
        for t in range(4):
            k8 = 8.0 * KL[j + 1, t]
            dg = 1.0 + k8 * near[t]
            r = scale / dg
            DG[j, t] = dg
            CL[j + 1, t] = tile_of(BN, j, t) * r
            WL[j, t] = k8 * r

    local_stage(lambda n: [KL[n, t] for t in range(4)], lambda n, t: KH[n, t], fine_a)

    recv_all(b_next, has_prev)
    recv_all(b_prev, has_next)

    def halo_a(j, i, near):
        scale = jnp.where(
            side0,
            jnp.where(half0, land(prev_tile, j), land(prev_tile, j + 32)),
            jnp.where(half0, land(next_tile, j), land(next_tile, j + 32)),
        ) * 0.8
        for t in range(4):
            k8 = 8.0 * KH[j + 1, t]
            r = scale / (1.0 + k8 * near[t])
            CH[j + 1, t] = tile_of(BHN, j, t) * r
            WH[j, t] = k8 * r

    halo_stage(lambda n: [KH[n, t] for t in range(4)], lambda n, t: KL[n, t], halo_a)
    pad_halo(CH)

    MS[1] = mass_total(0)
    mass_start(1)

    def fine_b(j, i, near):
        for t in range(4):
            FL[j + 1, t] = 1.2 * CL[j + 1, t] + WL[j, t] * near[t]

    def halo_b(j, i, near):
        for t in range(4):
            FH[j + 1, t] = 1.2 * CH[j + 1, t] + WH[j, t] * near[t]

    def product(k, f):
        return lambda n: [k[n, t] * f[n, t] for t in range(4)]

    def product1(k, f):
        return lambda n, t: k[n, t] * f[n, t]

    local_stage(product(KL, CL), product1(KH, CH), fine_b)
    halo_stage(product(KH, CH), product1(KL, CL), halo_b)
    pad_halo(FH)

    def fine_c(j, i, near):
        parts = [
            (CL[j + 1, t] - 0.8 * FL[j + 1, t] + WL[j, t] * near[t]) * DG[j, t] for t in range(4)
        ]
        RS[pl.ds(pl.multiple_of((j // 4) * 8, 8), 8), pl.ds(128 * (i % 4), 128)] = (parts[0] + parts[1]) + (parts[2] + parts[3])

    local_stage(product(KL, FL), product1(KH, FH), fine_c)
    PC[2] = exact_dot(RS[...], squeeze).reshape(16, 8, 128) * GQ[...]
    for copy, there, _ in p_copies:
        start_all([copy], there)

    MS[2] = mass_total(1)
    mass_start(2)

    for copy, _, back in q_copies + p_copies:
        recv_all([copy], back)

    for slot in range(5):
        UC[pl.ds(1, 16), slot] = PC[slot]

    def coarse_sweep(old, new, slots):
        def sa(q):
            u = {slot: old[q + 1, slot] for slot in slots}
            s = []
            for slot in slots:
                up, down = rs(u[slot], 1), rs(u[slot], -1)
                if slot - 1 in u:
                    up = jnp.where(m0, rs(u[slot - 1], -3), up)
                if slot + 1 in u:
                    down = jnp.where(m3, rs(u[slot + 1], 3), down)
                s.append(up + down)
            return s, [u[slot] + 0.5 * x for slot, x in zip(slots, s)]

        def finalize(q, i, near):
            for n, slot in enumerate(slots):
                new[q + 1, slot] = 0.2 * old[q + 1, slot] + PC[slot, q] + QC[slot, q] * near[n]

        along(0, 16, sa, finalize, begin(sa, 0), 16)

    wide = range(5)
    narrow = range(1, 4)
    coarse_sweep(UC, UP, wide)
    coarse_sweep(UP, UC, wide)
    coarse_sweep(UC, UP, wide)
    coarse_sweep(UP, UC, wide)
    coarse_sweep(UC, UP, narrow)
    coarse_sweep(UP, UC, narrow)
    coarse_sweep(UC, UP, narrow)

    own = UP[pl.ds(1, 16), 2] * ICK[pl.ds(0, 16)]
    beside = []
    for q in range(8):
        above0, below0 = UP[q + 1, 1], UP[q + 1, 3]
        above1, below1 = UP[q + 9, 1], UP[q + 9, 3]
        rows = jnp.where(
            half0,
            jnp.where(side0, rs(above0, -3), rs(below0, 1)),
            jnp.where(side0, rs(above1, -1), rs(below1, 3)),
        )
        beside.append(rows * ICK[16 + q])
    OH_up = exact_dot(own.reshape(128, 128), stretch)
    RS[...] = OH_up
    OH_side = exact_dot(jnp.concatenate(beside, axis=0), stretch)

    def add_local(q, _):
        for i in range(4):
            up = RS[pl.ds(pl.multiple_of(q * 8, 8), 8), pl.ds(128 * i, 128)]
            for t in range(4):
                FL[4 * q + i + 1, t] = FL[4 * q + i + 1, t] + up
        return 0

    lax.fori_loop(0, 16, add_local, 0)
    RS[pl.ds(0, 64), :] = OH_side

    def add_halo(q, _):
        for i in range(4):
            up = RS[pl.ds(pl.multiple_of(q * 8, 8), 8), pl.ds(128 * i, 128)]
            for t in range(4):
                FH[4 * q + i + 1, t] = FH[4 * q + i + 1, t] + up
        return 0

    lax.fori_loop(0, 8, add_halo, 0)
    pad_halo(FH)

    def fine_d(j, i, near):
        for t in range(4):
            GL[j + 1, t] = 0.2 * FL[j + 1, t] + CL[j + 1, t] + WL[j, t] * near[t]

    def halo_d(j, i, near):
        for t in (0, 3):
            GH[j + 1, t] = 0.2 * FH[j + 1, t] + CH[j + 1, t] + WH[j, t] * near[t]

    local_stage(product(KL, FL), product1(KH, FH), fine_d)
    halo_stage(product(KH, FH), product1(KL, FL), halo_d)
    for t in (0, 3):
        GH[0, t] = jnp.where(half0, 0.0, rs(GH[32, t], 2))
        GH[33, t] = jnp.where(half0, rs(GH[1, t], -2), 0.0)

    mass = jnp.sum(mass_total(2))
    cells = float(2 * 16 * 8192) * ntiles * ncls
    ratio = jnp.where(sub < 4, target_ref[0], target_ref[1]) * cells / jnp.full((8, 128), mass, F32)

    def fine_e(j, i, near):
        level = ratio * land(row_tile, j)
        for t in range(4):
            f = 0.2 * GL[j + 1, t] + CL[j + 1, t] + WL[j, t] * near[t]
            OH[j, pl.ds(t, 8, stride=4), :] = f
            OF[j, pl.ds(t, 8, stride=4), :] = tile_of(SN, j, t) * level / jnp.maximum(f, FLOOR_LEVEL)

    local_stage(product(KL, GL), product1(KH, GH), fine_e)

    sent_all(k_next + b_next, has_next)
    sent_all(k_prev + b_prev, has_prev)
    for copy, there, _ in q_copies + p_copies:
        sent_all([copy], there)
    for stage in range(3):
        for r in range(1, sizes[stage]):
            mass_copy(stage, r).wait_send()


def write_out(heat, flow, heat_out, flow_out, sem):
    copies = [
        pltpu.make_async_copy(
            x.at[:, pl.ds(16 * c + 8 * rt, 8), :], out.at[c, rt], sem.at[4 * n + 2 * c + rt]
        )
        for n, (x, out) in enumerate(((heat, heat_out), (flow, flow_out)))
        for c in range(2)
        for rt in range(2)
    ]
    for copy in copies:
        copy.start()
    for copy in copies:
        copy.wait()


def solution(mesh):
    ntiles, ncls = mesh.shape["tiles"], mesh.shape["cls"]

    def tiles_view(x):
        return x.reshape(2, 2, 8, 64, 128).transpose(0, 1, 3, 2, 4)

    def rows_view(x):
        return x.transpose(0, 1, 3, 2, 4).reshape(2, 16, 8192)

    def on_device(scaling, source, speed, tile_mask, target):
        def body(*refs):
            kernel(ntiles, ncls, *refs)

        def vmem(*shape):
            return pltpu.VMEM(shape, F32)

        dma = pltpu.SemaphoreType.DMA
        any_space = pl.BlockSpec(memory_space=pl.ANY)
        heat, flow = pl.pallas_call(
            body,
            out_shape=[pltpu.VMEM((64, 32, 128), F32)] * 2,
            in_specs=[any_space] * 5,
            out_specs=[pl.BlockSpec(memory_space=pltpu.VMEM)] * 2,
            scratch_shapes=[
                vmem(66, 32, 128), vmem(64, 32, 128), vmem(64, 32, 128),
                vmem(34, 32, 128), vmem(32, 32, 128),
                vmem(66, 4, 8, 128), vmem(66, 4, 8, 128), vmem(64, 4, 8, 128), vmem(64, 4, 8, 128),
                vmem(66, 4, 8, 128), vmem(66, 4, 8, 128),
                vmem(34, 4, 8, 128), vmem(34, 4, 8, 128), vmem(32, 4, 8, 128),
                vmem(34, 4, 8, 128), vmem(34, 4, 8, 128),
                vmem(128, 512),
                vmem(18, 8, 128), vmem(16, 8, 128), vmem(24, 8, 128),
                vmem(5, 16, 8, 128), vmem(5, 16, 8, 128),
                vmem(18, 5, 8, 128), vmem(18, 5, 8, 128),
                vmem(3, 8, 128), vmem(20, 8, 128),
                pltpu.SMEM((8, 32), jnp.int32), pltpu.SMEM((2,), F32),
                dma((14,)),
                dma((8,)), dma((8,)), dma((8,)), dma((8,)),
                dma((4,)), dma((4,)), dma((4,)), dma((4,)),
                dma((20,)), dma((20,)),
            ],
            compiler_params=pltpu.CompilerParams(
                collective_id=0, has_side_effects=True, vmem_limit_bytes=48 * 2**20
            ),
        )(*(
            pltpu.with_memory_space_constraint(x, pltpu.HBM)
            for x in (tile_mask, target, tiles_view(scaling), tiles_view(source), tiles_view(speed))
        ))
        heat, flow = pl.pallas_call(
            write_out,
            out_shape=[jax.ShapeDtypeStruct((2, 2, 64, 8, 128), F32)] * 2,
            in_specs=[any_space] * 2,
            out_specs=[any_space] * 2,
            scratch_shapes=[dma((8,))],
            compiler_params=pltpu.CompilerParams(vmem_limit_bytes=4 * 2**20),
        )(heat, flow)
        return rows_view(heat), rows_view(flow)

    placed = (P("cls", "tiles", None), P("cls", "tiles", None), P("cls", "tiles", None), P(), P("cls"))
    return jax.shard_map(
        on_device,
        mesh=mesh,
        in_specs=placed,
        out_specs=(P("cls", "tiles", None), P("cls", "tiles", None)),
        check_vma=False,
    )
```

```python
import jax
import jax.numpy as jnp
from jax import lax
from jax.experimental import pallas as pl
from jax.experimental.pallas import tpu as pltpu
from jax.sharding import PartitionSpec as P

MESH = pl.DeviceIdType.MESH
F32 = jnp.float32
BF16 = jnp.bfloat16
FLOOR_LEVEL = 0.25
TS = 256


class View:
    def __init__(self, ref, c):
        self.ref, self.c = ref, c

    def _at(self, index):
        if index is Ellipsis:
            return (self.c,)
        return (self.c,) + (index if isinstance(index, tuple) else (index,))

    def __getitem__(self, index):
        return self.ref[self._at(index)]

    def __setitem__(self, index, value):
        self.ref[self._at(index)] = value


def kernel(
    ntiles, ncls,
    mask_in, target_in, b_in, src_in, k_in,
    OH, OF,
    KN, BN, SN, KHN, BHN, KL, CL, WL, DG, FL, GL, KH, CH, WH, FH, GH, RS, RH, CK, GQ, ICK, PC, QC, UC, UP, MS, MR,
    mask_ref, target_ref,
    sem_in, k_send, k_recv, b_send, b_recv, q_send, q_recv, p_send, p_recv, m_send, m_recv,
):
    me = lax.axis_index("tiles")
    cl = lax.axis_index("cls")
    has_prev, has_next = me > 0, me < ntiles - 1
    has_prev2, has_next2 = me > 1, me < ntiles - 2

    sub = lax.broadcasted_iota(jnp.int32, (8, 128), 0)
    lane = lax.broadcasted_iota(jnp.int32, (8, 128), 1)
    s4 = sub & 3
    m0, m3 = s4 == 0, s4 == 3
    low_half = sub < 4
    quarter_even = s4 < 2
    side0 = (sub & 1) == 0
    lane0, lane127 = lane == 0, lane == 127
    zero = jnp.zeros((8, 128), F32)

    def rs(x, n):
        return pltpu.roll(x, n % 8, 0)

    def rl(x, n):
        return pltpu.roll(x, n % 128, 1)

    low = me % 8
    mid = me // 8 % 2
    high = me // 16
    place = 2 * mid + cl

    def mass_peer(stage, r):
        if stage == 0:
            return {"tiles": me - low + (low + r) % 8, "cls": cl}
        if stage == 1:
            other = (place + r) % 4
            return {"tiles": me + 8 * (other // 2 - mid), "cls": other % 2}
        return {"tiles": me + 16 * ((high + r) % 8 - high), "cls": cl}

    sizes = (8, 4, 8)
    starts = (0, 8, 12)

    barrier = pltpu.get_barrier_semaphore()

    def greet(there):
        pl.semaphore_signal(barrier, inc=1, device_id=there, device_id_type=MESH)

    for step, there in ((-1, has_prev), (1, has_next), (-2, has_prev2), (2, has_next2)):
        @pl.when(there)
        def _():
            greet({"tiles": me + step})
    for stage in range(3):
        for r in range(1, sizes[stage]):
            greet(mass_peer(stage, r))

    def load_copies(hbm, vmem, s, c):
        return [
            pltpu.make_async_copy(
                hbm.at[c, rt, pl.ds(32 * half, 32)],
                vmem.at[c, :, pl.ds(16 * half + 8 * rt, 8), :],
                sem_in.at[s * 8 + 4 * c + 2 * half + rt],
            )
            for half in range(2)
            for rt in range(2)
        ]

    k_loads = [load_copies(k_in, KN, 0, c) for c in range(2)]
    b_loads = [load_copies(b_in, BN, 1, c) for c in range(2)]
    s_loads = load_copies(src_in, SN, 2, 0) + load_copies(src_in, SN, 2, 1)
    small_loads = [
        pltpu.make_async_copy(mask_in, mask_ref, sem_in.at[24]),
        pltpu.make_async_copy(target_in, target_ref, sem_in.at[25]),
    ]
    for copy in k_loads[0] + k_loads[1] + s_loads + small_loads + b_loads[0] + b_loads[1]:
        copy.start()

    one = jnp.int32(1)
    nil = jnp.int32(0)
    greeted = 17
    for there in (has_prev, has_next, has_prev2, has_next2):
        greeted = greeted + jnp.where(there, one, nil)
    pl.semaphore_wait(barrier, greeted)

    def halo_copies(hbm, vmem, c, send, recv):
        to_next, to_prev = [], []
        for q in range(4):
            n = 8 * c + q
            to_next.append(pltpu.make_async_remote_copy(
                src_ref=hbm.at[c, 1, pl.ds(16 * q, 16), pl.ds(4, 4), :],
                dst_ref=vmem.at[c, :, pl.ds(8 * q, 4), :],
                send_sem=send.at[n], recv_sem=recv.at[n],
                device_id={"tiles": me + 1}, device_id_type=MESH))
            to_prev.append(pltpu.make_async_remote_copy(
                src_ref=hbm.at[c, 0, pl.ds(16 * q, 16), pl.ds(0, 4), :],
                dst_ref=vmem.at[c, :, pl.ds(8 * q + 4, 4), :],
                send_sem=send.at[4 + n], recv_sem=recv.at[4 + n],
                device_id={"tiles": me - 1}, device_id_type=MESH))
        return to_next, to_prev

    def start_all(copies, there):
        @pl.when(there)
        def _():
            for copy in copies:
                copy.start()

    def recv_all(copies, there):
        @pl.when(there)
        def _():
            for copy in copies:
                copy.wait_recv()

    def sent_all(copies, there):
        @pl.when(there)
        def _():
            for copy in copies:
                copy.wait_send()

    k_halo = [halo_copies(k_in, KHN, c, k_send, k_recv) for c in range(2)]
    b_halo = [halo_copies(b_in, BHN, c, b_send, b_recv) for c in range(2)]
    for c in range(2):
        for to_next, to_prev in (k_halo[c], b_halo[c]):
            start_all(to_next, has_next)
            start_all(to_prev, has_prev)

    def outside(first, there):
        @pl.when(jnp.logical_not(there))
        def _():
            for c in range(2):
                for q in range(4):
                    KHN[c, :, pl.ds(8 * q + first, 4), :] = jnp.zeros((16, 4, 128), F32)
                    BHN[c, :, pl.ds(8 * q + first, 4), :] = jnp.zeros((16, 4, 128), F32)

    outside(0, has_prev)
    outside(4, has_next)

    def clear(slot, there):
        @pl.when(jnp.logical_not(there))
        def _():
            for c in range(2):
                PC[c, slot] = jnp.zeros((8, 8, 128), F32)
                QC[c, slot] = jnp.zeros((8, 8, 128), F32)

    clear(0, has_prev2)
    clear(1, has_prev)
    clear(3, has_next)
    clear(4, has_next2)

    def mass_copy(stage, r):
        return pltpu.make_async_remote_copy(
            src_ref=MS.at[stage], dst_ref=MR.at[starts[stage] + r],
            send_sem=m_send.at[starts[stage] + r], recv_sem=m_recv.at[starts[stage] + r],
            device_id=mass_peer(stage, r), device_id_type=MESH)

    def mass_start(stage):
        for r in range(1, sizes[stage]):
            mass_copy(stage, r).start()

    def mass_total(stage):
        total = MS[stage]
        for r in range(1, sizes[stage]):
            mass_copy(stage, r).wait_recv()
        for r in range(1, sizes[stage]):
            total = total + MR[starts[stage] + r]
        return total

    for copy in s_loads + small_loads:
        copy.wait()

    def add_source(n, sums):
        return tuple(
            sums[i] + SN[i // 4, n, pl.ds(8 * (i % 4), 8), :] for i in range(8)
        )

    sums = lax.fori_loop(0, 32, add_source, (zero,) * 8)
    total = sums[0]
    for part in sums[1:]:
        total = total + part
    MS[0] = total
    mass_start(0)

    row_tile = me * 16 // TS
    prev_tile = jnp.maximum(me * 16 - 1, 0) // TS
    next_tile = jnp.minimum(me * 16 + 16, ntiles * 16 - 1) // TS

    def land(row, block):
        return mask_ref[row, block // 2].astype(F32)

    def land_local(j):
        return jnp.where(low_half, land(row_tile, j), land(row_tile, j + 32))

    def land_halo(j):
        def pick(row):
            return jnp.where(
                low_half,
                jnp.where(quarter_even, land(row, j), land(row, j + 16)),
                jnp.where(quarter_even, land(row, j + 32), land(row, j + 48)),
            )
        return jnp.where(side0, pick(prev_tile), pick(next_tile))

    def along(first, count, sa, finalize, carry):
        def body(n, carry):
            for i in range(count):
                j = first + n + i
                before, s, right, left = carry
                s_next, a_next = sa(j + 1)
                right_next = [rl(x, 1) for x in a_next]
                left_next = [rl(x, -1) for x in a_next]
                near = [
                    s[t] + jnp.where(lane0, before[t], right[t]) + jnp.where(lane127, left_next[t], left[t])
                    for t in range(len(s))
                ]
                finalize(j, i, near)
                carry = (right, s_next, right_next, left_next)
            return carry

        return lax.fori_loop(0, 1, body, carry)

    def begin(sa, first):
        _, a_before = sa(first - 1)
        s, a = sa(first)
        return ([rl(x, 1) for x in a_before], s, [rl(x, 1) for x in a], [rl(x, -1) for x in a])

    def sums_of(u, up0, down3):
        s = [up0 + u[1], u[0] + u[2], u[1] + u[3], u[2] + down3]
        return s, [u[t] + 0.5 * s[t] for t in range(4)]

    def local_stage(u_at, edge_at, finalize):
        def sa_of(odd):
            def sa(j):
                u = u_at(j + 1)
                h = j - 16 * odd + 1
                above, below = edge_at(h, 3), edge_at(h, 0)
                if odd:
                    above = rs(above, -2)
                else:
                    below = rs(below, 2)
                return sums_of(
                    u, jnp.where(m0, above, rs(u[3], 1)), jnp.where(m3, below, rs(u[0], -1))
                )
            return sa

        carry = begin(sa_of(0), 0)
        carry = along(0, 16, sa_of(0), finalize, carry)
        along(16, 16, sa_of(1), finalize, carry)

    def halo_stage(u_at, local_at, finalize):
        def sa(j):
            u = u_at(j + 1)
            up0 = jnp.where(m3, local_at(j + 17, 3), rs(local_at(j + 1, 3), -2))
            down3 = jnp.where(m0, local_at(j + 1, 0), rs(local_at(j + 17, 0), 2))
            return sums_of(u, up0, down3)

        along(0, 16, sa, finalize, begin(sa, 0))

    def pad_local(ref):
        for t in range(4):
            ref[0, t] = jnp.where(low_half, 0.0, rs(ref[32, t], 4))
            ref[33, t] = jnp.where(low_half, rs(ref[1, t], 4), 0.0)

    def pad_halo(ref, tiles=(0, 1, 2, 3)):
        for t in tiles:
            ref[0, t] = jnp.where(sub < 2, 0.0, rs(ref[16, t], 2))
            ref[17, t] = jnp.where(sub < 6, rs(ref[1, t], -2), 0.0)

    def tile_of(ref, n, t):
        return ref[n, pl.ds(t, 8, stride=4), :]

    fine_lane = lax.broadcasted_iota(jnp.int32, (512, 128), 0)
    coarse_lane = lax.broadcasted_iota(jnp.int32, (512, 128), 1)
    squeeze = jnp.where(fine_lane // 4 == coarse_lane, 1.0, 0.0).astype(BF16)
    fine_lane2 = lax.broadcasted_iota(jnp.int32, (128, 512), 1)
    coarse_lane2 = lax.broadcasted_iota(jnp.int32, (128, 512), 0)
    stretch = jnp.where(fine_lane2 // 4 == coarse_lane2, 1.0, 0.0).astype(BF16)

    def exact_dot(x, y):
        high_part = x.astype(BF16)
        rest = x - high_part.astype(F32)
        middle = rest.astype(BF16)
        low_part = (rest - middle.astype(F32)).astype(BF16)
        out = jnp.dot(high_part, y, preferred_element_type=F32)
        out = out + jnp.dot(middle, y, preferred_element_type=F32)
        return out + jnp.dot(low_part, y, preferred_element_type=F32)

    def product(k, f):
        return lambda n: [k[n, t] * f[n, t] for t in range(4)]

    def product1(k, f):
        return lambda n, t: k[n, t] * f[n, t]

    def band_speed(c):
        for copy in k_loads[c]:
            copy.wait()
        kn, kl, rsum = View(KN, c), View(KL, c), View(RS, c)

        def body(q, _):
            for i in range(4):
                tiles = [tile_of(kn, 4 * q + i, t) for t in range(4)]
                for t in range(4):
                    kl[4 * q + i + 1, t] = tiles[t]
                rsum[pl.ds(pl.multiple_of(q * 8, 8), 8), pl.ds(128 * i, 128)] = (tiles[0] + tiles[1]) + (tiles[2] + tiles[3])
            return 0

        lax.fori_loop(0, 8, body, 0)
        pad_local(kl)
        CK[c] = (exact_dot(rsum[...], squeeze) * 0.0625).reshape(8, 8, 128)

    def coarse_copies(ref, c, send, recv):
        out = []
        for n, (step, there, back) in enumerate(
            ((1, has_next, has_prev), (-1, has_prev, has_next), (2, has_next2, has_prev2), (-2, has_prev2, has_next2))
        ):
            out.append((pltpu.make_async_remote_copy(
                src_ref=ref.at[c, 2], dst_ref=ref.at[c, 2 - step],
                send_sem=send.at[4 * c + n], recv_sem=recv.at[4 * c + n],
                device_id={"tiles": me + step}, device_id_type=MESH), there, back))
        return out

    q_copies = [coarse_copies(QC, c, q_send, q_recv) for c in range(2)]
    p_copies = [coarse_copies(PC, c, p_send, p_recv) for c in range(2)]

    def down(c):
        kl, cl_, wl, dgr, fl = View(KL, c), View(CL, c), View(WL, c), View(DG, c), View(FL, c)
        kh, ch, wh, fh = View(KH, c), View(CH, c), View(WH, c), View(FH, c)
        khn, bn, bhn, rsum = View(KHN, c), View(BN, c), View(BHN, c), View(RS, c)

        recv_all(k_halo[c][0], has_prev)
        recv_all(k_halo[c][1], has_next)

        def halo_speed(q, _):
            for i in range(4):
                tiles = [tile_of(khn, 4 * q + i, t) for t in range(4)]
                for t in range(4):
                    kh[4 * q + i + 1, t] = tiles[t]
                rsum[pl.ds(pl.multiple_of(q * 8, 8), 8), pl.ds(128 * i, 128)] = (tiles[0] + tiles[1]) + (tiles[2] + tiles[3])
            return 0

        lax.fori_loop(0, 4, halo_speed, 0)
        pad_halo(kh)
        ckh = (exact_dot(rsum[pl.ds(0, 32), :], squeeze) * 0.0625).reshape(4, 8, 128)

        def coarse_sa(q):
            ck = CK[c, q]
            h = ckh[q % 4]
            if q < 4:
                above, below = h, rs(h, 2)
            else:
                above, below = rs(h, -2), h
            s = jnp.where(m0, above, rs(ck, 1)) + jnp.where(m3, below, rs(ck, -1))
            return s, ck + 0.5 * s

        pairs = [coarse_sa(q) for q in range(8)]
        right = [rl(a, 1) for _, a in pairs]
        left = [rl(a, -1) for _, a in pairs]
        right_pad = jnp.where(low_half, 0.0, rs(right[7], 4))
        left_pad = jnp.where(low_half, rs(left[0], 4), 0.0)
        for q in range(8):
            ck = CK[c, q]
            near = (
                pairs[q][0]
                + jnp.where(lane0, right[q - 1] if q else right_pad, right[q])
                + jnp.where(lane127, left[q + 1] if q < 7 else left_pad, left[q])
            )
            land_q = jnp.where(lane < 64, land_local(4 * q), land_local(4 * q + 2))
            g = ck * land_q / (16.0 + 32.0 * ck * near)
            GQ[c, q] = g
            QC[c, 2, q] = 25.6 * ck * g
            ICK[c, q] = 1.0 / ck
        for q in range(4):
            ICK[c, 8 + q] = 1.0 / jnp.maximum(ckh[q], 1e-30)
        for copy, there, _ in q_copies[c]:
            start_all([copy], there)

        for copy in b_loads[c]:
            copy.wait()

        def fine_a(j, i, near):
            scale = 0.8 * land_local(j)
            for t in range(4):
                k8 = 8.0 * kl[j + 1, t]
                dg = 1.0 + k8 * near[t]
                r = scale / dg
                dgr[j, t] = dg
                cl_[j + 1, t] = tile_of(bn, j, t) * r
                wl[j, t] = k8 * r

        local_stage(lambda n: [kl[n, t] for t in range(4)], lambda n, t: kh[n, t], fine_a)
        pad_local(cl_)

        recv_all(b_halo[c][0], has_prev)
        recv_all(b_halo[c][1], has_next)

        def halo_a(j, i, near):
            scale = 0.8 * land_halo(j)
            for t in range(4):
                k8 = 8.0 * kh[j + 1, t]
                r = scale / (1.0 + k8 * near[t])
                ch[j + 1, t] = tile_of(bhn, j, t) * r
                wh[j, t] = k8 * r

        halo_stage(lambda n: [kh[n, t] for t in range(4)], lambda n, t: kl[n, t], halo_a)
        pad_halo(ch)

        def fine_b(j, i, near):
            for t in range(4):
                fl[j + 1, t] = 1.2 * cl_[j + 1, t] + wl[j, t] * near[t]

        def halo_b(j, i, near):
            for t in range(4):
                fh[j + 1, t] = 1.2 * ch[j + 1, t] + wh[j, t] * near[t]

        local_stage(product(kl, cl_), product1(kh, ch), fine_b)
        halo_stage(product(kh, ch), product1(kl, cl_), halo_b)
        pad_local(fl)
        pad_halo(fh)

        def fine_c(j, i, near):
            parts = [
                (cl_[j + 1, t] - 0.8 * fl[j + 1, t] + wl[j, t] * near[t]) * dgr[j, t] for t in range(4)
            ]
            rsum[pl.ds(pl.multiple_of((j // 4) * 8, 8), 8), pl.ds(128 * (i % 4), 128)] = (parts[0] + parts[1]) + (parts[2] + parts[3])

        local_stage(product(kl, fl), product1(kh, fh), fine_c)
        PC[c, 2] = exact_dot(rsum[...], squeeze).reshape(8, 8, 128) * GQ[c]
        for copy, there, _ in p_copies[c]:
            start_all([copy], there)

    def coarse_sweep(c, old, new, slots):
        def sa(q):
            u = {slot: old[q + 1, slot] for slot in slots}
            s = []
            for slot in slots:
                up, dn = rs(u[slot], 1), rs(u[slot], -1)
                if slot - 1 in u:
                    up = jnp.where(m0, rs(u[slot - 1], -3), up)
                if slot + 1 in u:
                    dn = jnp.where(m3, rs(u[slot + 1], 3), dn)
                s.append(up + dn)
            return s, [u[slot] + 0.5 * x for slot, x in zip(slots, s)]

        def finalize(q, i, near):
            for n, slot in enumerate(slots):
                new[q + 1, slot] = 0.2 * old[q + 1, slot] + PC[c, slot, q] + QC[c, slot, q] * near[n]

        along(0, 8, sa, finalize, begin(sa, 0))
        coarse_pads(new, slots)

    def coarse_pads(ref, slots):
        for slot in slots:
            ref[0, slot] = jnp.where(low_half, 0.0, rs(ref[8, slot], 4))
            ref[9, slot] = jnp.where(low_half, rs(ref[1, slot], 4), 0.0)

    wide = range(5)
    narrow = range(1, 4)

    def up(c):
        kl, cl_, wl, fl, gl = View(KL, c), View(CL, c), View(WL, c), View(FL, c), View(GL, c)
        kh, ch, wh, fh, gh = View(KH, c), View(CH, c), View(WH, c), View(FH, c), View(GH, c)
        uc, uq, rsum, rhal = View(UC, c), View(UP, c), View(RS, c), View(RH, c)
        for copy, _, back in q_copies[c] + p_copies[c]:
            recv_all([copy], back)
        for slot in range(5):
            uc[pl.ds(1, 8), slot] = PC[c, slot]
        coarse_pads(uc, wide)

        def two_sweeps(n, _):
            coarse_sweep(c, uc, uq, wide)
            coarse_sweep(c, uq, uc, wide)
            return 0

        lax.fori_loop(0, 2, two_sweeps, 0)
        coarse_sweep(c, uc, uq, narrow)
        coarse_sweep(c, uq, uc, narrow)
        coarse_sweep(c, uc, uq, narrow)

        own = uq[pl.ds(1, 8), 2] * ICK[c, pl.ds(0, 8)]
        beside = []
        for q in range(4):
            above0, below0 = uq[q + 1, 1], uq[q + 1, 3]
            above1, below1 = uq[q + 5, 1], uq[q + 5, 3]
            rows = jnp.where(
                quarter_even,
                jnp.where(side0, rs(above0, -3), rs(below0, 1)),
                jnp.where(side0, rs(above1, -1), rs(below1, 3)),
            )
            beside.append(rows * ICK[c, 8 + q])
        rsum[...] = exact_dot(own.reshape(64, 128), stretch)
        rhal[...] = exact_dot(jnp.concatenate(beside, axis=0), stretch)

        def add_up(count, field, part):
            def body(q, _):
                for i in range(4):
                    more = part[pl.ds(pl.multiple_of(q * 8, 8), 8), pl.ds(128 * i, 128)]
                    for t in range(4):
                        field[4 * q + i + 1, t] = field[4 * q + i + 1, t] + more
                return 0

            lax.fori_loop(0, count, body, 0)

        add_up(8, fl, rsum)
        add_up(4, fh, rhal)
        pad_local(fl)
        pad_halo(fh)

        def fine_d(j, i, near):
            for t in range(4):
                gl[j + 1, t] = 0.2 * fl[j + 1, t] + cl_[j + 1, t] + wl[j, t] * near[t]

        def halo_d(j, i, near):
            for t in (0, 3):
                gh[j + 1, t] = 0.2 * fh[j + 1, t] + ch[j + 1, t] + wh[j, t] * near[t]

        local_stage(product(kl, fl), product1(kh, fh), fine_d)
        halo_stage(product(kh, fh), product1(kl, fl), halo_d)
        pad_local(gl)
        pad_halo(gh, (0, 3))

    def last(c, mass):
        kl, cl_, wl, gl = View(KL, c), View(CL, c), View(WL, c), View(GL, c)
        kh, gh, sn, oh, of = View(KH, c), View(GH, c), View(SN, c), View(OH, c), View(OF, c)
        cells = float(2 * 16 * 8192) * ntiles * ncls
        ratio = jnp.full((8, 128), target_ref[c] * cells, F32) / mass

        def fine_e(j, i, near):
            level = ratio * land_local(j)
            for t in range(4):
                f = 0.2 * gl[j + 1, t] + cl_[j + 1, t] + wl[j, t] * near[t]
                oh[j, pl.ds(t, 8, stride=4), :] = f
                of[j, pl.ds(t, 8, stride=4), :] = tile_of(sn, j, t) * level / jnp.maximum(f, FLOOR_LEVEL)

        local_stage(product(kl, gl), product1(kh, gh), fine_e)

    band_speed(0)
    band_speed(1)
    down(0)
    MS[1] = mass_total(0)
    mass_start(1)
    down(1)
    MS[2] = mass_total(1)
    mass_start(2)
    up(0)
    up(1)
    mass = jnp.full((8, 128), jnp.sum(mass_total(2)), F32)
    last(0, mass)
    last(1, mass)

    for c in range(2):
        sent_all(k_halo[c][0] + b_halo[c][0], has_next)
        sent_all(k_halo[c][1] + b_halo[c][1], has_prev)
        for copy, there, _ in q_copies[c] + p_copies[c]:
            sent_all([copy], there)
    for stage in range(3):
        for r in range(1, sizes[stage]):
            mass_copy(stage, r).wait_send()


def write_out(heat, flow, heat_out, flow_out, sem):
    copies = [
        pltpu.make_async_copy(
            x.at[c, :, pl.ds(16 * half + 8 * rt, 8), :],
            out.at[c, rt, pl.ds(32 * half, 32)],
            sem.at[8 * n + 4 * c + 2 * half + rt],
        )
        for n, (x, out) in enumerate(((heat, heat_out), (flow, flow_out)))
        for c in range(2)
        for half in range(2)
        for rt in range(2)
    ]
    for copy in copies:
        copy.start()
    for copy in copies:
        copy.wait()


def solution(mesh):
    ntiles, ncls = mesh.shape["tiles"], mesh.shape["cls"]

    def tiles_view(x):
        return x.reshape(2, 2, 8, 64, 128).transpose(0, 1, 3, 2, 4)

    def rows_view(x):
        return x.transpose(0, 1, 3, 2, 4).reshape(2, 16, 8192)

    def on_device(scaling, source, speed, tile_mask, target):
        def body(*refs):
            kernel(ntiles, ncls, *refs)

        def vmem(*shape):
            return pltpu.VMEM(shape, F32)

        dma = pltpu.SemaphoreType.DMA
        any_space = pl.BlockSpec(memory_space=pl.ANY)
        heat, flow = pl.pallas_call(
            body,
            out_shape=[pltpu.VMEM((2, 32, 32, 128), F32)] * 2,
            in_specs=[any_space] * 5,
            out_specs=[pl.BlockSpec(memory_space=pltpu.VMEM)] * 2,
            scratch_shapes=[
                vmem(2, 32, 32, 128), vmem(2, 32, 32, 128), vmem(2, 32, 32, 128),
                vmem(2, 16, 32, 128), vmem(2, 16, 32, 128),
                vmem(2, 34, 4, 8, 128), vmem(2, 34, 4, 8, 128),
                vmem(2, 32, 4, 8, 128), vmem(2, 32, 4, 8, 128),
                vmem(2, 34, 4, 8, 128), vmem(2, 34, 4, 8, 128),
                vmem(2, 18, 4, 8, 128), vmem(2, 18, 4, 8, 128), vmem(2, 16, 4, 8, 128),
                vmem(2, 18, 4, 8, 128), vmem(2, 18, 4, 8, 128),
                vmem(2, 64, 512), vmem(2, 32, 512),
                vmem(2, 8, 8, 128), vmem(2, 8, 8, 128), vmem(2, 12, 8, 128),
                vmem(2, 5, 8, 8, 128), vmem(2, 5, 8, 8, 128),
                vmem(2, 10, 5, 8, 128), vmem(2, 10, 5, 8, 128),
                vmem(3, 8, 128), vmem(20, 8, 128),
                pltpu.SMEM((8, 32), jnp.int32), pltpu.SMEM((2,), F32),
                dma((26,)),
                dma((16,)), dma((16,)), dma((16,)), dma((16,)),
                dma((8,)), dma((8,)), dma((8,)), dma((8,)),
                dma((20,)), dma((20,)),
            ],
            compiler_params=pltpu.CompilerParams(
                collective_id=0, has_side_effects=True, vmem_limit_bytes=48 * 2**20
            ),
        )(*(
            pltpu.with_memory_space_constraint(x, pltpu.HBM)
            for x in (tile_mask, target, tiles_view(scaling), tiles_view(source), tiles_view(speed))
        ))
        heat, flow = pl.pallas_call(
            write_out,
            out_shape=[jax.ShapeDtypeStruct((2, 2, 64, 8, 128), F32)] * 2,
            in_specs=[any_space] * 2,
            out_specs=[any_space] * 2,
            scratch_shapes=[dma((16,))],
            compiler_params=pltpu.CompilerParams(vmem_limit_bytes=4 * 2**20),
        )(heat, flow)
        return rows_view(heat), rows_view(flow)

    placed = (P("cls", "tiles", None), P("cls", "tiles", None), P("cls", "tiles", None), P(), P("cls"))
    return jax.shard_map(
        on_device,
        mesh=mesh,
        in_specs=placed,
        out_specs=(P("cls", "tiles", None), P("cls", "tiles", None)),
        check_vma=False,
    )
```

```python
import jax
import jax.numpy as jnp
from jax import lax
from jax.experimental import pallas as pl
from jax.experimental.pallas import tpu as pltpu
from jax.sharding import PartitionSpec as P

MESH = pl.DeviceIdType.MESH
F32 = jnp.float32
BF16 = jnp.bfloat16
FLOOR_LEVEL = 0.25
TS = 256


class View:
    def __init__(self, ref, c):
        self.ref, self.c = ref, c

    def _at(self, index):
        if index is Ellipsis:
            return (self.c,)
        return (self.c,) + (index if isinstance(index, tuple) else (index,))

    def __getitem__(self, index):
        return self.ref[self._at(index)]

    def __setitem__(self, index, value):
        self.ref[self._at(index)] = value


def stencil():
    sub = lax.broadcasted_iota(jnp.int32, (8, 128), 0)
    lane = lax.broadcasted_iota(jnp.int32, (8, 128), 1)
    s4 = sub & 3
    m0, m3 = s4 == 0, s4 == 3
    low_half = sub < 4
    quarter_even = s4 < 2
    side0 = (sub & 1) == 0
    lane0, lane127 = lane == 0, lane == 127
    zero = jnp.zeros((8, 128), F32)

    def rs(x, n):
        return pltpu.roll(x, n % 8, 0)

    def rl(x, n):
        return pltpu.roll(x, n % 128, 1)

    def along(first, count, sa, finalize, carry):
        def body(n, carry):
            for i in range(count):
                j = first + n + i
                before, s, right, left = carry
                s_next, a_next = sa(j + 1)
                right_next = [rl(x, 1) for x in a_next]
                left_next = [rl(x, -1) for x in a_next]
                near = [
                    s[t] + jnp.where(lane0, before[t], right[t]) + jnp.where(lane127, left_next[t], left[t])
                    for t in range(len(s))
                ]
                finalize(j, i, near)
                carry = (right, s_next, right_next, left_next)
            return carry

        return lax.fori_loop(0, 1, body, carry)

    def begin(sa, first):
        _, a_before = sa(first - 1)
        s, a = sa(first)
        return ([rl(x, 1) for x in a_before], s, [rl(x, 1) for x in a], [rl(x, -1) for x in a])

    def sums_of(u, up0, down3):
        s = [up0 + u[1], u[0] + u[2], u[1] + u[3], u[2] + down3]
        return s, [u[t] + 0.5 * s[t] for t in range(4)]

    def local_stage(u_at, edge_at, finalize):
        def sa_of(odd):
            def sa(j):
                u = u_at(j + 1)
                h = j - 16 * odd + 1
                above, below = edge_at(h, 3), edge_at(h, 0)
                if odd:
                    above = rs(above, -2)
                else:
                    below = rs(below, 2)
                return sums_of(
                    u, jnp.where(m0, above, rs(u[3], 1)), jnp.where(m3, below, rs(u[0], -1))
                )
            return sa

        carry = begin(sa_of(0), 0)
        carry = along(0, 16, sa_of(0), finalize, carry)
        along(16, 16, sa_of(1), finalize, carry)

    def halo_stage(u_at, local_at, finalize):
        def sa(j):
            u = u_at(j + 1)
            up0 = jnp.where(m3, local_at(j + 17, 3), rs(local_at(j + 1, 3), -2))
            down3 = jnp.where(m0, local_at(j + 1, 0), rs(local_at(j + 17, 0), 2))
            return sums_of(u, up0, down3)

        along(0, 16, sa, finalize, begin(sa, 0))

    def pad_local(ref):
        for t in range(4):
            ref[0, t] = jnp.where(low_half, 0.0, rs(ref[32, t], 4))
            ref[33, t] = jnp.where(low_half, rs(ref[1, t], 4), 0.0)

    def pad_halo(ref, tiles=(0, 1, 2, 3)):
        for t in tiles:
            ref[0, t] = jnp.where(sub < 2, 0.0, rs(ref[16, t], 2))
            ref[17, t] = jnp.where(sub < 6, rs(ref[1, t], -2), 0.0)

    def tile_of(ref, n, t):
        return ref[n, pl.ds(t, 8, stride=4), :]

    def product(k, f):
        return lambda n: [k[n, t] * f[n, t] for t in range(4)]

    def product1(k, f):
        return lambda n, t: k[n, t] * f[n, t]

    return (
        sub, lane, s4, m0, m3, low_half, quarter_even, side0, lane0, lane127, zero, rs,
        rl, local_stage, halo_stage, pad_local, pad_halo, tile_of, product, product1,
    )


def kernel(
    ntiles, ncls,
    mask_in, target_in, b_in, src_in, k_in,
    KL, CL, WL, GL, KH, GH, SN, LV,
    KN, BN, KHN, BHN, DG, FL, CH, WH, FH, RS, RH, CK, GQ, ICK, PC, QC, MS, MR,
    mask_ref, target_ref,
    sem_in, k_send, k_recv, b_send, b_recv, q_send, q_recv, p_send, p_recv, m_send, m_recv,
):
    me = lax.axis_index("tiles")
    cl = lax.axis_index("cls")
    has_prev, has_next = me > 0, me < ntiles - 1
    has_prev2, has_next2 = me > 1, me < ntiles - 2

    (
        sub, lane, s4, m0, m3, low_half, quarter_even, side0, lane0, lane127, zero, rs,
        rl, local_stage, halo_stage, pad_local, pad_halo, tile_of, product, product1,
    ) = stencil()

    low = me % 8
    mid = me // 8 % 2
    high = me // 16
    place = 2 * mid + cl

    def mass_peer(stage, r):
        if stage == 0:
            return {"tiles": me - low + (low + r) % 8, "cls": cl}
        if stage == 1:
            other = (place + r) % 4
            return {"tiles": me + 8 * (other // 2 - mid), "cls": other % 2}
        return {"tiles": me + 16 * ((high + r) % 8 - high), "cls": cl}

    sizes = (8, 4, 8)
    starts = (0, 8, 12)

    barrier = pltpu.get_barrier_semaphore()

    def greet(there):
        pl.semaphore_signal(barrier, inc=1, device_id=there, device_id_type=MESH)

    for step, there in ((-1, has_prev), (1, has_next), (-2, has_prev2), (2, has_next2)):
        @pl.when(there)
        def _():
            greet({"tiles": me + step})
    for stage in range(3):
        for r in range(1, sizes[stage]):
            greet(mass_peer(stage, r))

    def load_copies(hbm, vmem, s, c):
        return [
            pltpu.make_async_copy(
                hbm.at[c, rt, pl.ds(32 * half, 32)],
                vmem.at[c, :, pl.ds(16 * half + 8 * rt, 8), :],
                sem_in.at[s * 8 + 4 * c + 2 * half + rt],
            )
            for half in range(2)
            for rt in range(2)
        ]

    k_loads = [load_copies(k_in, KN, 0, c) for c in range(2)]
    b_loads = [load_copies(b_in, BN, 1, c) for c in range(2)]
    s_loads = load_copies(src_in, SN, 2, 0) + load_copies(src_in, SN, 2, 1)
    small_loads = [
        pltpu.make_async_copy(mask_in, mask_ref, sem_in.at[24]),
        pltpu.make_async_copy(target_in, target_ref, sem_in.at[25]),
    ]
    for copy in k_loads[0] + k_loads[1] + s_loads + small_loads + b_loads[0] + b_loads[1]:
        copy.start()

    one = jnp.int32(1)
    nil = jnp.int32(0)
    greeted = 17
    for there in (has_prev, has_next, has_prev2, has_next2):
        greeted = greeted + jnp.where(there, one, nil)
    pl.semaphore_wait(barrier, greeted)

    def halo_copies(hbm, vmem, c, send, recv):
        to_next, to_prev = [], []
        for q in range(4):
            n = 8 * c + q
            to_next.append(pltpu.make_async_remote_copy(
                src_ref=hbm.at[c, 1, pl.ds(16 * q, 16), pl.ds(4, 4), :],
                dst_ref=vmem.at[c, :, pl.ds(8 * q, 4), :],
                send_sem=send.at[n], recv_sem=recv.at[n],
                device_id={"tiles": me + 1}, device_id_type=MESH))
            to_prev.append(pltpu.make_async_remote_copy(
                src_ref=hbm.at[c, 0, pl.ds(16 * q, 16), pl.ds(0, 4), :],
                dst_ref=vmem.at[c, :, pl.ds(8 * q + 4, 4), :],
                send_sem=send.at[4 + n], recv_sem=recv.at[4 + n],
                device_id={"tiles": me - 1}, device_id_type=MESH))
        return to_next, to_prev

    def start_all(copies, there):
        @pl.when(there)
        def _():
            for copy in copies:
                copy.start()

    def recv_all(copies, there):
        @pl.when(there)
        def _():
            for copy in copies:
                copy.wait_recv()

    def sent_all(copies, there):
        @pl.when(there)
        def _():
            for copy in copies:
                copy.wait_send()

    k_halo = [halo_copies(k_in, KHN, c, k_send, k_recv) for c in range(2)]
    b_halo = [halo_copies(b_in, BHN, c, b_send, b_recv) for c in range(2)]
    for c in range(2):
        for to_next, to_prev in (k_halo[c], b_halo[c]):
            start_all(to_next, has_next)
            start_all(to_prev, has_prev)

    def outside(first, there):
        @pl.when(jnp.logical_not(there))
        def _():
            for c in range(2):
                for q in range(4):
                    KHN[c, :, pl.ds(8 * q + first, 4), :] = jnp.zeros((16, 4, 128), F32)
                    BHN[c, :, pl.ds(8 * q + first, 4), :] = jnp.zeros((16, 4, 128), F32)

    outside(0, has_prev)
    outside(4, has_next)

    def clear(slot, there):
        @pl.when(jnp.logical_not(there))
        def _():
            for c in range(2):
                PC[c, slot] = jnp.zeros((8, 8, 128), F32)
                QC[c, slot] = jnp.zeros((8, 8, 128), F32)

    clear(0, has_prev2)
    clear(1, has_prev)
    clear(3, has_next)
    clear(4, has_next2)

    def mass_copy(stage, r):
        return pltpu.make_async_remote_copy(
            src_ref=MS.at[stage], dst_ref=MR.at[starts[stage] + r],
            send_sem=m_send.at[starts[stage] + r], recv_sem=m_recv.at[starts[stage] + r],
            device_id=mass_peer(stage, r), device_id_type=MESH)

    def mass_start(stage):
        for r in range(1, sizes[stage]):
            mass_copy(stage, r).start()

    def mass_total(stage):
        total = MS[stage]
        for r in range(1, sizes[stage]):
            mass_copy(stage, r).wait_recv()
        for r in range(1, sizes[stage]):
            total = total + MR[starts[stage] + r]
        return total

    for copy in s_loads + small_loads:
        copy.wait()

    def add_source(n, sums):
        return tuple(
            sums[i] + SN[i // 4, n, pl.ds(8 * (i % 4), 8), :] for i in range(8)
        )

    sums = lax.fori_loop(0, 32, add_source, (zero,) * 8)
    total = sums[0]
    for part in sums[1:]:
        total = total + part
    MS[0] = total
    mass_start(0)

    row_tile = me * 16 // TS
    prev_tile = jnp.maximum(me * 16 - 1, 0) // TS
    next_tile = jnp.minimum(me * 16 + 16, ntiles * 16 - 1) // TS

    def land(row, block):
        return mask_ref[row, block // 2].astype(F32)

    def land_local(j):
        return jnp.where(low_half, land(row_tile, j), land(row_tile, j + 32))

    def land_halo(j):
        def pick(row):
            return jnp.where(
                low_half,
                jnp.where(quarter_even, land(row, j), land(row, j + 16)),
                jnp.where(quarter_even, land(row, j + 32), land(row, j + 48)),
            )
        return jnp.where(side0, pick(prev_tile), pick(next_tile))

    fine_lane = lax.broadcasted_iota(jnp.int32, (512, 128), 0)
    coarse_lane = lax.broadcasted_iota(jnp.int32, (512, 128), 1)
    squeeze = jnp.where(fine_lane // 4 == coarse_lane, 1.0, 0.0).astype(BF16)
    fine_lane2 = lax.broadcasted_iota(jnp.int32, (128, 512), 1)
    coarse_lane2 = lax.broadcasted_iota(jnp.int32, (128, 512), 0)
    stretch = jnp.where(fine_lane2 // 4 == coarse_lane2, 1.0, 0.0).astype(BF16)

    def exact_dot(x, y):
        high_part = x.astype(BF16)
        rest = x - high_part.astype(F32)
        middle = rest.astype(BF16)
        low_part = (rest - middle.astype(F32)).astype(BF16)
        out = jnp.dot(high_part, y, preferred_element_type=F32)
        out = out + jnp.dot(middle, y, preferred_element_type=F32)
        return out + jnp.dot(low_part, y, preferred_element_type=F32)

    def band_speed(c):
        for copy in k_loads[c]:
            copy.wait()
        kn, kl, rsum = View(KN, c), View(KL, c), View(RS, c)

        def body(q, _):
            for i in range(4):
                tiles = [tile_of(kn, 4 * q + i, t) for t in range(4)]
                for t in range(4):
                    kl[4 * q + i + 1, t] = tiles[t]
                rsum[pl.ds(pl.multiple_of(q * 8, 8), 8), pl.ds(128 * i, 128)] = (tiles[0] + tiles[1]) + (tiles[2] + tiles[3])
            return 0

        lax.fori_loop(0, 8, body, 0)
        pad_local(kl)
        CK[c] = (exact_dot(rsum[...], squeeze) * 0.0625).reshape(8, 8, 128)

    def coarse_copies(ref, c, send, recv):
        out = []
        for n, (step, there, back) in enumerate(
            ((1, has_next, has_prev), (-1, has_prev, has_next), (2, has_next2, has_prev2), (-2, has_prev2, has_next2))
        ):
            out.append((pltpu.make_async_remote_copy(
                src_ref=ref.at[c, 2], dst_ref=ref.at[c, 2 - step],
                send_sem=send.at[4 * c + n], recv_sem=recv.at[4 * c + n],
                device_id={"tiles": me + step}, device_id_type=MESH), there, back))
        return out

    q_copies = [coarse_copies(QC, c, q_send, q_recv) for c in range(2)]
    p_copies = [coarse_copies(PC, c, p_send, p_recv) for c in range(2)]

    def down(c):
        kl, cl_, wl, dgr, fl = View(KL, c), View(CL, c), View(WL, c), View(DG, c), View(FL, c)
        kh, ch, wh, fh = View(KH, c), View(CH, c), View(WH, c), View(FH, c)
        khn, bn, bhn, rsum = View(KHN, c), View(BN, c), View(BHN, c), View(RS, c)

        recv_all(k_halo[c][0], has_prev)
        recv_all(k_halo[c][1], has_next)

        def halo_speed(q, _):
            for i in range(4):
                tiles = [tile_of(khn, 4 * q + i, t) for t in range(4)]
                for t in range(4):
                    kh[4 * q + i + 1, t] = tiles[t]
                rsum[pl.ds(pl.multiple_of(q * 8, 8), 8), pl.ds(128 * i, 128)] = (tiles[0] + tiles[1]) + (tiles[2] + tiles[3])
            return 0

        lax.fori_loop(0, 4, halo_speed, 0)
        pad_halo(kh)
        ckh = (exact_dot(rsum[pl.ds(0, 32), :], squeeze) * 0.0625).reshape(4, 8, 128)

        def coarse_sa(q):
            ck = CK[c, q]
            h = ckh[q % 4]
            if q < 4:
                above, below = h, rs(h, 2)
            else:
                above, below = rs(h, -2), h
            s = jnp.where(m0, above, rs(ck, 1)) + jnp.where(m3, below, rs(ck, -1))
            return s, ck + 0.5 * s

        pairs = [coarse_sa(q) for q in range(8)]
        right = [rl(a, 1) for _, a in pairs]
        left = [rl(a, -1) for _, a in pairs]
        right_pad = jnp.where(low_half, 0.0, rs(right[7], 4))
        left_pad = jnp.where(low_half, rs(left[0], 4), 0.0)
        for q in range(8):
            ck = CK[c, q]
            near = (
                pairs[q][0]
                + jnp.where(lane0, right[q - 1] if q else right_pad, right[q])
                + jnp.where(lane127, left[q + 1] if q < 7 else left_pad, left[q])
            )
            land_q = jnp.where(lane < 64, land_local(4 * q), land_local(4 * q + 2))
            g = ck * land_q / (16.0 + 32.0 * ck * near)
            GQ[c, q] = g
            QC[c, 2, q] = 25.6 * ck * g
            ICK[c, q] = 1.0 / ck
        for q in range(4):
            ICK[c, 8 + q] = 1.0 / jnp.maximum(ckh[q], 1e-30)
        for copy, there, _ in q_copies[c]:
            start_all([copy], there)

        for copy in b_loads[c]:
            copy.wait()

        def fine_a(j, i, near):
            scale = 0.8 * land_local(j)
            for t in range(4):
                k8 = 8.0 * kl[j + 1, t]
                dg = 1.0 + k8 * near[t]
                r = scale / dg
                dgr[j, t] = dg
                cl_[j + 1, t] = tile_of(bn, j, t) * r
                wl[j, t] = k8 * r

        local_stage(lambda n: [kl[n, t] for t in range(4)], lambda n, t: kh[n, t], fine_a)
        pad_local(cl_)

        recv_all(b_halo[c][0], has_prev)
        recv_all(b_halo[c][1], has_next)

        def halo_a(j, i, near):
            scale = 0.8 * land_halo(j)
            for t in range(4):
                k8 = 8.0 * kh[j + 1, t]
                r = scale / (1.0 + k8 * near[t])
                ch[j + 1, t] = tile_of(bhn, j, t) * r
                wh[j, t] = k8 * r

        halo_stage(lambda n: [kh[n, t] for t in range(4)], lambda n, t: kl[n, t], halo_a)
        pad_halo(ch)

        def fine_b(j, i, near):
            for t in range(4):
                fl[j + 1, t] = 1.2 * cl_[j + 1, t] + wl[j, t] * near[t]

        def halo_b(j, i, near):
            for t in range(4):
                fh[j + 1, t] = 1.2 * ch[j + 1, t] + wh[j, t] * near[t]

        local_stage(product(kl, cl_), product1(kh, ch), fine_b)
        halo_stage(product(kh, ch), product1(kl, cl_), halo_b)
        pad_local(fl)
        pad_halo(fh)

        def fine_c(j, i, near):
            parts = [
                (cl_[j + 1, t] - 0.8 * fl[j + 1, t] + wl[j, t] * near[t]) * dgr[j, t] for t in range(4)
            ]
            rsum[pl.ds(pl.multiple_of((j // 4) * 8, 8), 8), pl.ds(128 * (i % 4), 128)] = (parts[0] + parts[1]) + (parts[2] + parts[3])

        local_stage(product(kl, fl), product1(kh, fh), fine_c)
        PC[c, 2] = exact_dot(rsum[...], squeeze).reshape(8, 8, 128) * GQ[c]
        for copy, there, _ in p_copies[c]:
            start_all([copy], there)

    def coarse_sweep(c, u, slots):
        new = {}
        for slot in slots:
            sums, right, left = [], [], []
            for q in range(8):
                above, below = rs(u[slot][q], 1), rs(u[slot][q], -1)
                if slot > 0:
                    above = jnp.where(m0, rs(u[slot - 1][q], -3), above)
                if slot < 4:
                    below = jnp.where(m3, rs(u[slot + 1][q], 3), below)
                s = above + below
                a = u[slot][q] + 0.5 * s
                sums.append(s)
                right.append(rl(a, 1))
                left.append(rl(a, -1))
            right_pad = jnp.where(low_half, 0.0, rs(right[7], 4))
            left_pad = jnp.where(low_half, rs(left[0], 4), 0.0)
            new[slot] = [
                0.2 * u[slot][q] + PC[c, slot, q] + QC[c, slot, q] * (
                    sums[q]
                    + jnp.where(lane0, right[q - 1] if q else right_pad, right[q])
                    + jnp.where(lane127, left[q + 1] if q < 7 else left_pad, left[q])
                )
                for q in range(8)
            ]
        return {**u, **new}

    def up(c):
        kl, cl_, wl, fl, gl = View(KL, c), View(CL, c), View(WL, c), View(FL, c), View(GL, c)
        kh, ch, wh, fh, gh = View(KH, c), View(CH, c), View(WH, c), View(FH, c), View(GH, c)
        rsum, rhal = View(RS, c), View(RH, c)
        for copy, _, back in q_copies[c] + p_copies[c]:
            recv_all([copy], back)
        u = {slot: [PC[c, slot, q] for q in range(8)] for slot in range(5)}
        for slots in (range(5),) * 4 + (range(1, 4),) * 3:
            u = coarse_sweep(c, u, slots)

        own = jnp.concatenate([u[2][q] * ICK[c, q] for q in range(8)], axis=0)
        beside = []
        for q in range(4):
            above0, below0 = u[1][q], u[3][q]
            above1, below1 = u[1][q + 4], u[3][q + 4]
            rows = jnp.where(
                quarter_even,
                jnp.where(side0, rs(above0, -3), rs(below0, 1)),
                jnp.where(side0, rs(above1, -1), rs(below1, 3)),
            )
            beside.append(rows * ICK[c, 8 + q])
        rsum[...] = exact_dot(own, stretch)
        rhal[...] = exact_dot(jnp.concatenate(beside, axis=0), stretch)

        def add_up(count, field, part):
            def body(q, _):
                for i in range(4):
                    more = part[pl.ds(pl.multiple_of(q * 8, 8), 8), pl.ds(128 * i, 128)]
                    for t in range(4):
                        field[4 * q + i + 1, t] = field[4 * q + i + 1, t] + more
                return 0

            lax.fori_loop(0, count, body, 0)

        add_up(8, fl, rsum)
        add_up(4, fh, rhal)
        pad_local(fl)
        pad_halo(fh)

        def fine_d(j, i, near):
            for t in range(4):
                gl[j + 1, t] = 0.2 * fl[j + 1, t] + cl_[j + 1, t] + wl[j, t] * near[t]

        def halo_d(j, i, near):
            for t in (0, 3):
                gh[j + 1, t] = 0.2 * fh[j + 1, t] + ch[j + 1, t] + wh[j, t] * near[t]

        local_stage(product(kl, fl), product1(kh, fh), fine_d)
        halo_stage(product(kh, fh), product1(kl, fl), halo_d)
        pad_local(gl)
        pad_halo(gh, (0, 3))

    band_speed(0)
    band_speed(1)
    down(0)
    MS[1] = mass_total(0)
    mass_start(1)
    down(1)
    MS[2] = mass_total(1)
    mass_start(2)
    up(0)
    up(1)
    mass = jnp.full((8, 128), jnp.sum(mass_total(2)), F32)
    cells = float(2 * 16 * 8192) * ntiles * ncls
    for c in range(2):
        ratio = jnp.full((8, 128), target_ref[c] * cells, F32) / mass
        for j in range(32):
            LV[c, j] = ratio * land_local(j)

    for c in range(2):
        sent_all(k_halo[c][0] + b_halo[c][0], has_next)
        sent_all(k_halo[c][1] + b_halo[c][1], has_prev)
        for copy, there, _ in q_copies[c] + p_copies[c]:
            sent_all([copy], there)
    for stage in range(3):
        for r in range(1, sizes[stage]):
            mass_copy(stage, r).wait_send()


def finish(KL, CL, WL, GL, KH, GH, SN, LV, heat_out, flow_out, OH, OF, sem):
    *_, local_stage, _, _, _, tile_of, product, product1 = stencil()
    copies = [
        [
            pltpu.make_async_copy(
                x.at[c, :, pl.ds(16 * half + 8 * rt, 8), :],
                out.at[c, rt, pl.ds(32 * half, 32)],
                sem.at[8 * n + 4 * c + 2 * half + rt],
            )
            for n, (x, out) in enumerate(((OH, heat_out), (OF, flow_out)))
            for half in range(2)
            for rt in range(2)
        ]
        for c in range(2)
    ]

    def last(c):
        kl, cl_, wl, gl = View(KL, c), View(CL, c), View(WL, c), View(GL, c)
        kh, gh, sn, oh, of = View(KH, c), View(GH, c), View(SN, c), View(OH, c), View(OF, c)

        def fine_e(j, i, near):
            level = LV[c, j]
            for t in range(4):
                f = 0.2 * gl[j + 1, t] + cl_[j + 1, t] + wl[j, t] * near[t]
                oh[j, pl.ds(t, 8, stride=4), :] = f
                of[j, pl.ds(t, 8, stride=4), :] = tile_of(sn, j, t) * level / jnp.maximum(f, FLOOR_LEVEL)

        local_stage(product(kl, gl), product1(kh, gh), fine_e)

    for c in range(2):
        last(c)
        for copy in copies[c]:
            copy.start()
    for c in range(2):
        for copy in copies[c]:
            copy.wait()


def solution(mesh):
    ntiles, ncls = mesh.shape["tiles"], mesh.shape["cls"]

    def tiles_view(x):
        return x.reshape(2, 2, 8, 64, 128).transpose(0, 1, 3, 2, 4)

    def rows_view(x):
        return x.transpose(0, 1, 3, 2, 4).reshape(2, 16, 8192)

    def on_device(scaling, source, speed, tile_mask, target):
        def body(*refs):
            kernel(ntiles, ncls, *refs)

        def vmem(*shape):
            return pltpu.VMEM(shape, F32)

        dma = pltpu.SemaphoreType.DMA
        any_space = pl.BlockSpec(memory_space=pl.ANY)
        parts = pl.pallas_call(
            body,
            out_shape=[
                vmem(2, 34, 4, 8, 128), vmem(2, 34, 4, 8, 128), vmem(2, 32, 4, 8, 128), vmem(2, 34, 4, 8, 128),
                vmem(2, 18, 4, 8, 128), vmem(2, 18, 4, 8, 128), vmem(2, 32, 32, 128), vmem(2, 32, 8, 128),
            ],
            in_specs=[any_space] * 5,
            out_specs=[pl.BlockSpec(memory_space=pltpu.VMEM)] * 8,
            scratch_shapes=[
                vmem(2, 32, 32, 128), vmem(2, 32, 32, 128),
                vmem(2, 16, 32, 128), vmem(2, 16, 32, 128),
                vmem(2, 32, 4, 8, 128), vmem(2, 34, 4, 8, 128),
                vmem(2, 18, 4, 8, 128), vmem(2, 16, 4, 8, 128), vmem(2, 18, 4, 8, 128),
                vmem(2, 64, 512), vmem(2, 32, 512),
                vmem(2, 8, 8, 128), vmem(2, 8, 8, 128), vmem(2, 12, 8, 128),
                vmem(2, 5, 8, 8, 128), vmem(2, 5, 8, 8, 128),
                vmem(3, 8, 128), vmem(20, 8, 128),
                pltpu.SMEM((8, 32), jnp.int32), pltpu.SMEM((2,), F32),
                dma((26,)),
                dma((16,)), dma((16,)), dma((16,)), dma((16,)),
                dma((8,)), dma((8,)), dma((8,)), dma((8,)),
                dma((20,)), dma((20,)),
            ],
            compiler_params=pltpu.CompilerParams(
                collective_id=0, has_side_effects=True, vmem_limit_bytes=48 * 2**20
            ),
        )(*(
            pltpu.with_memory_space_constraint(x, pltpu.HBM)
            for x in (tile_mask, target, tiles_view(scaling), tiles_view(source), tiles_view(speed))
        ))
        heat, flow = pl.pallas_call(
            finish,
            out_shape=[jax.ShapeDtypeStruct((2, 2, 64, 8, 128), F32)] * 2,
            in_specs=[pl.BlockSpec(memory_space=pltpu.VMEM)] * 8,
            out_specs=[any_space] * 2,
            scratch_shapes=[vmem(2, 32, 32, 128), vmem(2, 32, 32, 128), dma((16,))],
            compiler_params=pltpu.CompilerParams(vmem_limit_bytes=16 * 2**20),
        )(*parts)
        return rows_view(heat), rows_view(flow)

    placed = (P("cls", "tiles", None), P("cls", "tiles", None), P("cls", "tiles", None), P(), P("cls"))
    return jax.shard_map(
        on_device,
        mesh=mesh,
        in_specs=placed,
        out_specs=(P("cls", "tiles", None), P("cls", "tiles", None)),
        check_vma=False,
    )
```

```python
import jax
import jax.numpy as jnp
from jax import lax
from jax.experimental import pallas as pl
from jax.experimental.pallas import tpu as pltpu
from jax.sharding import PartitionSpec as P

MESH = pl.DeviceIdType.MESH
F32 = jnp.float32
BF16 = jnp.bfloat16
FLOOR_LEVEL = 0.25
TS = 256


class View:
    def __init__(self, ref, c):
        self.ref, self.c = ref, c

    def _at(self, index):
        if index is Ellipsis:
            return (self.c,)
        return (self.c,) + (index if isinstance(index, tuple) else (index,))

    def __getitem__(self, index):
        return self.ref[self._at(index)]

    def __setitem__(self, index, value):
        self.ref[self._at(index)] = value


def stencil():
    sub = lax.broadcasted_iota(jnp.int32, (8, 128), 0)
    lane = lax.broadcasted_iota(jnp.int32, (8, 128), 1)
    s4 = sub & 3
    m0, m3 = s4 == 0, s4 == 3
    low_half = sub < 4
    quarter_even = s4 < 2
    side0 = (sub & 1) == 0
    lane0, lane127 = lane == 0, lane == 127
    zero = jnp.zeros((8, 128), F32)

    def rs(x, n):
        return pltpu.roll(x, n % 8, 0)

    def rl(x, n):
        return pltpu.roll(x, n % 128, 1)

    def along(first, count, sa, finalize, carry):
        def body(n, carry):
            for i in range(count):
                j = first + n + i
                before, s, right, left = carry
                s_next, a_next = sa(j + 1)
                right_next = [rl(x, 1) for x in a_next]
                left_next = [rl(x, -1) for x in a_next]
                near = [
                    s[t] + jnp.where(lane0, before[t], right[t]) + jnp.where(lane127, left_next[t], left[t])
                    for t in range(len(s))
                ]
                finalize(j, i, near)
                carry = (right, s_next, right_next, left_next)
            return carry

        return lax.fori_loop(0, 1, body, carry)

    def begin(sa, first):
        _, a_before = sa(first - 1)
        s, a = sa(first)
        return ([rl(x, 1) for x in a_before], s, [rl(x, 1) for x in a], [rl(x, -1) for x in a])

    def sums_of(u, up0, down3):
        s = [up0 + u[1], u[0] + u[2], u[1] + u[3], u[2] + down3]
        return s, [u[t] + 0.5 * s[t] for t in range(4)]

    def local_stage(u_at, edge_at, finalize):
        def sa_of(odd):
            def sa(j):
                u = u_at(j + 1)
                h = j - 16 * odd + 1
                above, below = edge_at(h, 3), edge_at(h, 0)
                if odd:
                    above = rs(above, -2)
                else:
                    below = rs(below, 2)
                return sums_of(
                    u, jnp.where(m0, above, rs(u[3], 1)), jnp.where(m3, below, rs(u[0], -1))
                )
            return sa

        carry = begin(sa_of(0), 0)
        carry = along(0, 16, sa_of(0), finalize, carry)
        along(16, 16, sa_of(1), finalize, carry)

    def halo_stage(u_at, local_at, finalize):
        def sa(j):
            u = u_at(j + 1)
            up0 = jnp.where(m3, local_at(j + 17, 3), rs(local_at(j + 1, 3), -2))
            down3 = jnp.where(m0, local_at(j + 1, 0), rs(local_at(j + 17, 0), 2))
            return sums_of(u, up0, down3)

        along(0, 16, sa, finalize, begin(sa, 0))

    def pad_local(ref):
        for t in range(4):
            ref[0, t] = jnp.where(low_half, 0.0, rs(ref[32, t], 4))
            ref[33, t] = jnp.where(low_half, rs(ref[1, t], 4), 0.0)

    def pad_halo(ref, tiles=(0, 1, 2, 3)):
        for t in tiles:
            ref[0, t] = jnp.where(sub < 2, 0.0, rs(ref[16, t], 2))
            ref[17, t] = jnp.where(sub < 6, rs(ref[1, t], -2), 0.0)

    def tile_of(ref, n, t):
        return ref[n, pl.ds(t, 8, stride=4), :]

    def product(k, f):
        return lambda n: [k[n, t] * f[n, t] for t in range(4)]

    def product1(k, f):
        return lambda n, t: k[n, t] * f[n, t]

    return (
        sub, lane, s4, m0, m3, low_half, quarter_even, side0, lane0, lane127, zero, rs,
        rl, local_stage, halo_stage, pad_local, pad_halo, tile_of, product, product1,
    )


def kernel(
    ntiles, ncls,
    mask_in, target_in, b_in, src_in, k_in,
    KL, CL, WL, GL, KH, GH, SN, LV,
    KN, BN, KHN, BHN, DG, FL, CH, WH, FH, RS, RH, CK, GQ, ICK, PC, QC, MS, MR,
    mask_ref, target_ref,
    sem_in, k_send, k_recv, b_send, b_recv, q_send, q_recv, p_send, p_recv, m_send, m_recv,
):
    me = lax.axis_index("tiles")
    cl = lax.axis_index("cls")
    has_prev, has_next = me > 0, me < ntiles - 1
    has_prev2, has_next2 = me > 1, me < ntiles - 2

    (
        sub, lane, s4, m0, m3, low_half, quarter_even, side0, lane0, lane127, zero, rs,
        rl, local_stage, halo_stage, pad_local, pad_halo, tile_of, product, product1,
    ) = stencil()

    low = me % 8
    mid = me // 8 % 2
    high = me // 16
    place = 2 * mid + cl

    def mass_peer(stage, r):
        if stage == 0:
            return {"tiles": me - low + (low + r) % 8, "cls": cl}
        if stage == 1:
            other = (place + r) % 4
            return {"tiles": me + 8 * (other // 2 - mid), "cls": other % 2}
        return {"tiles": me + 16 * ((high + r) % 8 - high), "cls": cl}

    sizes = (8, 4, 8)
    starts = (0, 8, 12)

    barrier = pltpu.get_barrier_semaphore()

    def greet(there):
        pl.semaphore_signal(barrier, inc=1, device_id=there, device_id_type=MESH)

    for step, there in ((-1, has_prev), (1, has_next), (-2, has_prev2), (2, has_next2)):
        @pl.when(there)
        def _():
            greet({"tiles": me + step})
    for stage in range(3):
        for r in range(1, sizes[stage]):
            greet(mass_peer(stage, r))

    def load_copies(hbm, vmem, s, c):
        return [
            pltpu.make_async_copy(
                hbm.at[c, rt, pl.ds(32 * half, 32)],
                vmem.at[c, :, pl.ds(16 * half + 8 * rt, 8), :],
                sem_in.at[s * 8 + 4 * c + 2 * half + rt],
            )
            for half in range(2)
            for rt in range(2)
        ]

    k_loads = [load_copies(k_in, KN, 0, c) for c in range(2)]
    b_loads = [load_copies(b_in, BN, 1, c) for c in range(2)]
    s_loads = load_copies(src_in, SN, 2, 0) + load_copies(src_in, SN, 2, 1)
    small_loads = [
        pltpu.make_async_copy(mask_in, mask_ref, sem_in.at[24]),
        pltpu.make_async_copy(target_in, target_ref, sem_in.at[25]),
    ]
    for copy in k_loads[0] + k_loads[1] + s_loads + small_loads + b_loads[0] + b_loads[1]:
        copy.start()

    one = jnp.int32(1)
    nil = jnp.int32(0)
    greeted = 17
    for there in (has_prev, has_next, has_prev2, has_next2):
        greeted = greeted + jnp.where(there, one, nil)
    pl.semaphore_wait(barrier, greeted)

    def halo_copies(hbm, vmem, c, send, recv, rows):
        to_next, to_prev = [], []
        for q in range(4):
            n = 8 * c + q
            to_next.append(pltpu.make_async_remote_copy(
                src_ref=hbm.at[c, 1, pl.ds(16 * q, 16), pl.ds(8 - rows, rows), :],
                dst_ref=vmem.at[c, :, pl.ds(8 * q + 4 - rows, rows), :],
                send_sem=send.at[n], recv_sem=recv.at[n],
                device_id={"tiles": me + 1}, device_id_type=MESH))
            to_prev.append(pltpu.make_async_remote_copy(
                src_ref=hbm.at[c, 0, pl.ds(16 * q, 16), pl.ds(0, rows), :],
                dst_ref=vmem.at[c, :, pl.ds(8 * q + 4, rows), :],
                send_sem=send.at[4 + n], recv_sem=recv.at[4 + n],
                device_id={"tiles": me - 1}, device_id_type=MESH))
        return to_next, to_prev

    def start_all(copies, there):
        @pl.when(there)
        def _():
            for copy in copies:
                copy.start()

    def recv_all(copies, there):
        @pl.when(there)
        def _():
            for copy in copies:
                copy.wait_recv()

    def sent_all(copies, there):
        @pl.when(there)
        def _():
            for copy in copies:
                copy.wait_send()

    k_halo = [halo_copies(k_in, KHN, c, k_send, k_recv, 4) for c in range(2)]
    b_halo = [halo_copies(b_in, BHN, c, b_send, b_recv, 3) for c in range(2)]
    for c in range(2):
        for to_next, to_prev in (k_halo[c], b_halo[c]):
            start_all(to_next, has_next)
            start_all(to_prev, has_prev)

    for c in range(2):
        for q in range(4):
            for row in (8 * q, 8 * q + 7):
                BHN[c, :, pl.ds(row, 1), :] = jnp.zeros((16, 1, 128), F32)

    def outside(first, there):
        @pl.when(jnp.logical_not(there))
        def _():
            for c in range(2):
                for q in range(4):
                    KHN[c, :, pl.ds(8 * q + first, 4), :] = jnp.zeros((16, 4, 128), F32)
                    BHN[c, :, pl.ds(8 * q + first, 4), :] = jnp.zeros((16, 4, 128), F32)

    outside(0, has_prev)
    outside(4, has_next)

    def clear(slot, there):
        @pl.when(jnp.logical_not(there))
        def _():
            for c in range(2):
                PC[c, slot] = jnp.zeros((8, 8, 128), F32)
                QC[c, slot] = jnp.zeros((8, 8, 128), F32)

    clear(0, has_prev2)
    clear(1, has_prev)
    clear(3, has_next)
    clear(4, has_next2)

    def mass_copy(stage, r):
        return pltpu.make_async_remote_copy(
            src_ref=MS.at[stage], dst_ref=MR.at[starts[stage] + r],
            send_sem=m_send.at[starts[stage] + r], recv_sem=m_recv.at[starts[stage] + r],
            device_id=mass_peer(stage, r), device_id_type=MESH)

    def mass_start(stage):
        for r in range(1, sizes[stage]):
            mass_copy(stage, r).start()

    def mass_total(stage):
        total = MS[stage]
        for r in range(1, sizes[stage]):
            mass_copy(stage, r).wait_recv()
        for r in range(1, sizes[stage]):
            total = total + MR[starts[stage] + r]
        return total

    for copy in s_loads + small_loads:
        copy.wait()

    def add_source(n, sums):
        return tuple(
            sums[i] + SN[i // 4, n, pl.ds(8 * (i % 4), 8), :] for i in range(8)
        )

    sums = lax.fori_loop(0, 32, add_source, (zero,) * 8)
    total = sums[0]
    for part in sums[1:]:
        total = total + part
    MS[0] = total
    mass_start(0)

    row_tile = me * 16 // TS
    prev_tile = jnp.maximum(me * 16 - 1, 0) // TS
    next_tile = jnp.minimum(me * 16 + 16, ntiles * 16 - 1) // TS

    def land(row, block):
        return mask_ref[row, block // 2].astype(F32)

    def land_local(j):
        return jnp.where(low_half, land(row_tile, j), land(row_tile, j + 32))

    def land_halo(j):
        def pick(row):
            return jnp.where(
                low_half,
                jnp.where(quarter_even, land(row, j), land(row, j + 16)),
                jnp.where(quarter_even, land(row, j + 32), land(row, j + 48)),
            )
        return jnp.where(side0, pick(prev_tile), pick(next_tile))

    fine_lane = lax.broadcasted_iota(jnp.int32, (512, 128), 0)
    coarse_lane = lax.broadcasted_iota(jnp.int32, (512, 128), 1)
    squeeze = jnp.where(fine_lane // 4 == coarse_lane, 1.0, 0.0).astype(BF16)
    fine_lane2 = lax.broadcasted_iota(jnp.int32, (128, 512), 1)
    coarse_lane2 = lax.broadcasted_iota(jnp.int32, (128, 512), 0)
    stretch = jnp.where(fine_lane2 // 4 == coarse_lane2, 1.0, 0.0).astype(BF16)

    def exact_dot(x, y):
        high_part = x.astype(BF16)
        rest = x - high_part.astype(F32)
        middle = rest.astype(BF16)
        low_part = (rest - middle.astype(F32)).astype(BF16)
        out = jnp.dot(high_part, y, preferred_element_type=F32)
        out = out + jnp.dot(middle, y, preferred_element_type=F32)
        return out + jnp.dot(low_part, y, preferred_element_type=F32)

    def band_speed(c):
        for copy in k_loads[c]:
            copy.wait()
        kn, kl, rsum = View(KN, c), View(KL, c), View(RS, c)

        def body(q, _):
            for i in range(4):
                tiles = [tile_of(kn, 4 * q + i, t) for t in range(4)]
                for t in range(4):
                    kl[4 * q + i + 1, t] = tiles[t]
                rsum[pl.ds(pl.multiple_of(q * 8, 8), 8), pl.ds(128 * i, 128)] = (tiles[0] + tiles[1]) + (tiles[2] + tiles[3])
            return 0

        lax.fori_loop(0, 8, body, 0)
        pad_local(kl)
        CK[c] = (exact_dot(rsum[...], squeeze) * 0.0625).reshape(8, 8, 128)

    def coarse_copies(ref, c, send, recv):
        out = []
        for n, (step, there, back) in enumerate(
            ((1, has_next, has_prev), (-1, has_prev, has_next), (2, has_next2, has_prev2), (-2, has_prev2, has_next2))
        ):
            out.append((pltpu.make_async_remote_copy(
                src_ref=ref.at[c, 2], dst_ref=ref.at[c, 2 - step],
                send_sem=send.at[4 * c + n], recv_sem=recv.at[4 * c + n],
                device_id={"tiles": me + step}, device_id_type=MESH), there, back))
        return out

    q_copies = [coarse_copies(QC, c, q_send, q_recv) for c in range(2)]
    p_copies = [coarse_copies(PC, c, p_send, p_recv) for c in range(2)]

    def down(c):
        kl, cl_, wl, dgr, fl = View(KL, c), View(CL, c), View(WL, c), View(DG, c), View(FL, c)
        kh, ch, wh, fh = View(KH, c), View(CH, c), View(WH, c), View(FH, c)
        khn, bn, bhn, rsum = View(KHN, c), View(BN, c), View(BHN, c), View(RS, c)

        recv_all(k_halo[c][0], has_prev)
        recv_all(k_halo[c][1], has_next)

        def halo_speed(q, _):
            for i in range(4):
                tiles = [tile_of(khn, 4 * q + i, t) for t in range(4)]
                for t in range(4):
                    kh[4 * q + i + 1, t] = tiles[t]
                rsum[pl.ds(pl.multiple_of(q * 8, 8), 8), pl.ds(128 * i, 128)] = (tiles[0] + tiles[1]) + (tiles[2] + tiles[3])
            return 0

        lax.fori_loop(0, 4, halo_speed, 0)
        pad_halo(kh)
        ckh = (exact_dot(rsum[pl.ds(0, 32), :], squeeze) * 0.0625).reshape(4, 8, 128)

        def coarse_sa(q):
            ck = CK[c, q]
            h = ckh[q % 4]
            if q < 4:
                above, below = h, rs(h, 2)
            else:
                above, below = rs(h, -2), h
            s = jnp.where(m0, above, rs(ck, 1)) + jnp.where(m3, below, rs(ck, -1))
            return s, ck + 0.5 * s

        pairs = [coarse_sa(q) for q in range(8)]
        right = [rl(a, 1) for _, a in pairs]
        left = [rl(a, -1) for _, a in pairs]
        right_pad = jnp.where(low_half, 0.0, rs(right[7], 4))
        left_pad = jnp.where(low_half, rs(left[0], 4), 0.0)
        for q in range(8):
            ck = CK[c, q]
            near = (
                pairs[q][0]
                + jnp.where(lane0, right[q - 1] if q else right_pad, right[q])
                + jnp.where(lane127, left[q + 1] if q < 7 else left_pad, left[q])
            )
            land_q = jnp.where(lane < 64, land_local(4 * q), land_local(4 * q + 2))
            g = ck * land_q / (16.0 + 32.0 * ck * near)
            GQ[c, q] = g
            QC[c, 2, q] = 25.6 * ck * g
            ICK[c, q] = 1.0 / ck
        for q in range(4):
            ICK[c, 8 + q] = 1.0 / jnp.maximum(ckh[q], 1e-30)
        for copy, there, _ in q_copies[c]:
            start_all([copy], there)

        for copy in b_loads[c]:
            copy.wait()

        def fine_a(j, i, near):
            scale = 0.8 * land_local(j)
            for t in range(4):
                k8 = 8.0 * kl[j + 1, t]
                dg = 1.0 + k8 * near[t]
                r = scale / dg
                dgr[j, t] = dg
                cl_[j + 1, t] = tile_of(bn, j, t) * r
                wl[j, t] = k8 * r

        local_stage(lambda n: [kl[n, t] for t in range(4)], lambda n, t: kh[n, t], fine_a)
        pad_local(cl_)

        recv_all(b_halo[c][0], has_prev)
        recv_all(b_halo[c][1], has_next)

        def halo_a(j, i, near):
            scale = 0.8 * land_halo(j)
            for t in range(4):
                k8 = 8.0 * kh[j + 1, t]
                r = scale / (1.0 + k8 * near[t])
                ch[j + 1, t] = tile_of(bhn, j, t) * r
                wh[j, t] = k8 * r

        halo_stage(lambda n: [kh[n, t] for t in range(4)], lambda n, t: kl[n, t], halo_a)
        pad_halo(ch)

        def fine_b(j, i, near):
            for t in range(4):
                fl[j + 1, t] = 1.2 * cl_[j + 1, t] + wl[j, t] * near[t]

        def halo_b(j, i, near):
            for t in range(4):
                fh[j + 1, t] = 1.2 * ch[j + 1, t] + wh[j, t] * near[t]

        local_stage(product(kl, cl_), product1(kh, ch), fine_b)
        halo_stage(product(kh, ch), product1(kl, cl_), halo_b)
        pad_local(fl)
        pad_halo(fh)

        def fine_c(j, i, near):
            parts = [
                (cl_[j + 1, t] - 0.8 * fl[j + 1, t] + wl[j, t] * near[t]) * dgr[j, t] for t in range(4)
            ]
            rsum[pl.ds(pl.multiple_of((j // 4) * 8, 8), 8), pl.ds(128 * (i % 4), 128)] = (parts[0] + parts[1]) + (parts[2] + parts[3])

        local_stage(product(kl, fl), product1(kh, fh), fine_c)
        PC[c, 2] = exact_dot(rsum[...], squeeze).reshape(8, 8, 128) * GQ[c]
        for copy, there, _ in p_copies[c]:
            start_all([copy], there)

    def coarse_sweep(c, u, slots):
        new = {}
        for slot in slots:
            sums, right, left = [], [], []
            for q in range(8):
                above, below = rs(u[slot][q], 1), rs(u[slot][q], -1)
                if slot > 0:
                    above = jnp.where(m0, rs(u[slot - 1][q], -3), above)
                if slot < 4:
                    below = jnp.where(m3, rs(u[slot + 1][q], 3), below)
                s = above + below
                a = u[slot][q] + 0.5 * s
                sums.append(s)
                right.append(rl(a, 1))
                left.append(rl(a, -1))
            right_pad = jnp.where(low_half, 0.0, rs(right[7], 4))
            left_pad = jnp.where(low_half, rs(left[0], 4), 0.0)
            new[slot] = [
                0.2 * u[slot][q] + PC[c, slot, q] + QC[c, slot, q] * (
                    sums[q]
                    + jnp.where(lane0, right[q - 1] if q else right_pad, right[q])
                    + jnp.where(lane127, left[q + 1] if q < 7 else left_pad, left[q])
                )
                for q in range(8)
            ]
        return {**u, **new}

    def up(c):
        kl, cl_, wl, fl, gl = View(KL, c), View(CL, c), View(WL, c), View(FL, c), View(GL, c)
        kh, ch, wh, fh, gh = View(KH, c), View(CH, c), View(WH, c), View(FH, c), View(GH, c)
        rsum, rhal = View(RS, c), View(RH, c)
        for copy, _, back in q_copies[c] + p_copies[c]:
            recv_all([copy], back)
        u = {slot: [PC[c, slot, q] for q in range(8)] for slot in range(5)}
        for slots in (range(5),) * 4 + (range(1, 4),) * 3:
            u = coarse_sweep(c, u, slots)

        own = jnp.concatenate([u[2][q] * ICK[c, q] for q in range(8)], axis=0)
        beside = []
        for q in range(4):
            above0, below0 = u[1][q], u[3][q]
            above1, below1 = u[1][q + 4], u[3][q + 4]
            rows = jnp.where(
                quarter_even,
                jnp.where(side0, rs(above0, -3), rs(below0, 1)),
                jnp.where(side0, rs(above1, -1), rs(below1, 3)),
            )
            beside.append(rows * ICK[c, 8 + q])
        rsum[...] = exact_dot(own, stretch)
        rhal[...] = exact_dot(jnp.concatenate(beside, axis=0), stretch)

        def add_up(count, field, part):
            def body(q, _):
                for i in range(4):
                    more = part[pl.ds(pl.multiple_of(q * 8, 8), 8), pl.ds(128 * i, 128)]
                    for t in range(4):
                        field[4 * q + i + 1, t] = field[4 * q + i + 1, t] + more
                return 0

            lax.fori_loop(0, count, body, 0)

        add_up(8, fl, rsum)
        add_up(4, fh, rhal)
        pad_local(fl)
        pad_halo(fh)

        def fine_d(j, i, near):
            for t in range(4):
                gl[j + 1, t] = 0.2 * fl[j + 1, t] + cl_[j + 1, t] + wl[j, t] * near[t]

        def halo_d(j, i, near):
            for t in (0, 3):
                gh[j + 1, t] = 0.2 * fh[j + 1, t] + ch[j + 1, t] + wh[j, t] * near[t]

        local_stage(product(kl, fl), product1(kh, fh), fine_d)
        halo_stage(product(kh, fh), product1(kl, fl), halo_d)
        pad_local(gl)
        pad_halo(gh, (0, 3))

    band_speed(0)
    band_speed(1)
    down(0)
    MS[1] = mass_total(0)
    mass_start(1)
    down(1)
    MS[2] = mass_total(1)
    mass_start(2)
    up(0)
    up(1)
    mass = jnp.full((8, 128), jnp.sum(mass_total(2)), F32)
    cells = float(2 * 16 * 8192) * ntiles * ncls
    for c in range(2):
        ratio = jnp.full((8, 128), target_ref[c] * cells, F32) / mass
        for j in range(32):
            LV[c, j] = ratio * land_local(j)

    for c in range(2):
        sent_all(k_halo[c][0] + b_halo[c][0], has_next)
        sent_all(k_halo[c][1] + b_halo[c][1], has_prev)
        for copy, there, _ in q_copies[c] + p_copies[c]:
            sent_all([copy], there)
    for stage in range(3):
        for r in range(1, sizes[stage]):
            mass_copy(stage, r).wait_send()


def finish(KL, CL, WL, GL, KH, GH, SN, LV, heat_out, flow_out, OH, OF, sem):
    *_, local_stage, _, _, _, tile_of, product, product1 = stencil()
    copies = [
        [
            pltpu.make_async_copy(
                x.at[c, :, pl.ds(16 * half + 8 * rt, 8), :],
                out.at[c, rt, pl.ds(32 * half, 32)],
                sem.at[8 * n + 4 * c + 2 * half + rt],
            )
            for n, (x, out) in enumerate(((OH, heat_out), (OF, flow_out)))
            for half in range(2)
            for rt in range(2)
        ]
        for c in range(2)
    ]

    def last(c):
        kl, cl_, wl, gl = View(KL, c), View(CL, c), View(WL, c), View(GL, c)
        kh, gh, sn, oh, of = View(KH, c), View(GH, c), View(SN, c), View(OH, c), View(OF, c)

        def fine_e(j, i, near):
            level = LV[c, j]
            for t in range(4):
                f = 0.2 * gl[j + 1, t] + cl_[j + 1, t] + wl[j, t] * near[t]
                oh[j, pl.ds(t, 8, stride=4), :] = f
                of[j, pl.ds(t, 8, stride=4), :] = tile_of(sn, j, t) * level / jnp.maximum(f, FLOOR_LEVEL)

        local_stage(product(kl, gl), product1(kh, gh), fine_e)

    for c in range(2):
        last(c)
        for copy in copies[c]:
            copy.start()
    for c in range(2):
        for copy in copies[c]:
            copy.wait()


def solution(mesh):
    ntiles, ncls = mesh.shape["tiles"], mesh.shape["cls"]

    def tiles_view(x):
        return x.reshape(2, 2, 8, 64, 128).transpose(0, 1, 3, 2, 4)

    def rows_view(x):
        return x.transpose(0, 1, 3, 2, 4).reshape(2, 16, 8192)

    def on_device(scaling, source, speed, tile_mask, target):
        def body(*refs):
            kernel(ntiles, ncls, *refs)

        def vmem(*shape):
            return pltpu.VMEM(shape, F32)

        dma = pltpu.SemaphoreType.DMA
        any_space = pl.BlockSpec(memory_space=pl.ANY)
        parts = pl.pallas_call(
            body,
            out_shape=[
                vmem(2, 34, 4, 8, 128), vmem(2, 34, 4, 8, 128), vmem(2, 32, 4, 8, 128), vmem(2, 34, 4, 8, 128),
                vmem(2, 18, 4, 8, 128), vmem(2, 18, 4, 8, 128), vmem(2, 32, 32, 128), vmem(2, 32, 8, 128),
            ],
            in_specs=[any_space] * 5,
            out_specs=[pl.BlockSpec(memory_space=pltpu.VMEM)] * 8,
            scratch_shapes=[
                vmem(2, 32, 32, 128), vmem(2, 32, 32, 128),
                vmem(2, 16, 32, 128), vmem(2, 16, 32, 128),
                vmem(2, 32, 4, 8, 128), vmem(2, 34, 4, 8, 128),
                vmem(2, 18, 4, 8, 128), vmem(2, 16, 4, 8, 128), vmem(2, 18, 4, 8, 128),
                vmem(2, 64, 512), vmem(2, 32, 512),
                vmem(2, 8, 8, 128), vmem(2, 8, 8, 128), vmem(2, 12, 8, 128),
                vmem(2, 5, 8, 8, 128), vmem(2, 5, 8, 8, 128),
                vmem(3, 8, 128), vmem(20, 8, 128),
                pltpu.SMEM((8, 32), jnp.int32), pltpu.SMEM((2,), F32),
                dma((26,)),
                dma((16,)), dma((16,)), dma((16,)), dma((16,)),
                dma((8,)), dma((8,)), dma((8,)), dma((8,)),
                dma((20,)), dma((20,)),
            ],
            compiler_params=pltpu.CompilerParams(
                collective_id=0, has_side_effects=True, vmem_limit_bytes=48 * 2**20
            ),
        )(*(
            pltpu.with_memory_space_constraint(x, pltpu.HBM)
            for x in (tile_mask, target, tiles_view(scaling), tiles_view(source), tiles_view(speed))
        ))
        heat, flow = pl.pallas_call(
            finish,
            out_shape=[jax.ShapeDtypeStruct((2, 2, 64, 8, 128), F32)] * 2,
            in_specs=[pl.BlockSpec(memory_space=pltpu.VMEM)] * 8,
            out_specs=[any_space] * 2,
            scratch_shapes=[vmem(2, 32, 32, 128), vmem(2, 32, 32, 128), dma((16,))],
            compiler_params=pltpu.CompilerParams(vmem_limit_bytes=16 * 2**20),
        )(*parts)
        return rows_view(heat), rows_view(flow)

    placed = (P("cls", "tiles", None), P("cls", "tiles", None), P("cls", "tiles", None), P(), P("cls"))
    return jax.shard_map(
        on_device,
        mesh=mesh,
        in_specs=placed,
        out_specs=(P("cls", "tiles", None), P("cls", "tiles", None)),
        check_vma=False,
    )
```
